32 devices in a mesh: dp: 16 (over z, y, x), tensor: 2 (over core).
Axes of the slice: x: 2, y: 2, z: 4, core: 2. Of those that a mesh axis runs over, the one named last changes fastest.
Arguments:
- obs: bfloat16 [65536, 376], P('dp'), may hold values from -6 to 6
- action: bfloat16 [65536, 17], P('dp'), may hold values from -0.94921875 to 0.94921875
- next_obs: bfloat16 [65536, 376], P('dp'), may hold values from -6 to 6
- reward: float32 [65536], P('dp'), may hold values from -6 to 6
- terminal: int32 [65536], P('dp'), may hold values 0 or 1
- noise: float32 [65536, 17], P('dp'), may hold values from -4 to 4
- next_noise: float32 [65536, 17], P('dp'), may hold values from -4 to 4
- counts: int32 [16], P('dp'), may hold values from 2048 to 4096, as said below
- step_count: int32 [1], replicated, may hold values from 2 to 21
- a_w1: float32 [377, 256], P(None, 'tensor'), may hold values from -0.3125 to 0.3125
- a_w2: float32 [256, 256], P('tensor'), may hold values from -0.375 to 0.375
- a_head: float32 [257, 34], replicated, may hold values from -0.375 to 0.375
- c_w1: float32 [2, 394, 256], P(None, None, 'tensor'), may hold values from -0.3125 to 0.3125
- c_w2: float32 [2, 256, 256], P(None, 'tensor'), may hold values from -0.375 to 0.375
- c_head: float32 [2, 257, 2], replicated, may hold values from -0.375 to 0.375
- bias2: float32 [3, 256], replicated, may hold values from -1.5 to 1.5
- tc_w1: float32 [2, 394, 256], P(None, None, 'tensor'), may hold values from -0.3125 to 0.3125
- tc_w2: float32 [2, 256, 256], P(None, 'tensor'), may hold values from -0.375 to 0.375
- tc_head: float32 [2, 257, 2], replicated, may hold values from -0.375 to 0.375
- tc_bias2: float32 [2, 256], replicated, may hold values from -1.5 to 1.5
- a_w1_mom: float32 [2, 377, 256], P(None, None, 'tensor'), as said below
- a_w2_mom: float32 [2, 256, 256], P(None, 'tensor'), as said below
- a_head_mom: float32 [2, 257, 34], replicated, as said below
- c_w1_mom: float32 [2, 2, 394, 256], P(None, None, None, 'tensor'), as said below
- c_w2_mom: float32 [2, 2, 256, 256], P(None, None, 'tensor'), as said below
- c_head_mom: float32 [2, 2, 257, 2], replicated, as said below
- bias2_mom: float32 [2, 3, 256], replicated, as said below
- state: float32 [4], replicated, as said below
Outputs:
- a_w1_new: float32 [377, 256], P(None, 'tensor')
- a_w1_first: float32 [377, 256], P(None, 'tensor')
- a_w1_second: float32 [377, 256], P(None, 'tensor')
- a_w2_new: float32 [256, 256], P('tensor')
- a_w2_first: float32 [256, 256], P('tensor')
- a_w2_second: float32 [256, 256], P('tensor')
- a_head_new: float32 [257, 34], replicated
- a_head_first: float32 [257, 34], replicated
- a_head_second: float32 [257, 34], replicated
- c_w1_new: float32 [4, 394, 256], P(None, None, 'tensor')
- c_w1_first: float32 [2, 394, 256], P(None, None, 'tensor')
- c_w1_second: float32 [2, 394, 256], P(None, None, 'tensor')
- c_w2_new: float32 [4, 256, 256], P(None, 'tensor')
- c_w2_first: float32 [2, 256, 256], P(None, 'tensor')
- c_w2_second: float32 [2, 256, 256], P(None, 'tensor')
- c_head_new: float32 [4, 257, 2], replicated
- c_head_first: float32 [2, 257, 2], replicated
- c_head_second: float32 [2, 257, 2], replicated
- bias2_new: float32 [5, 256], replicated
- bias2_first: float32 [3, 256], replicated
- bias2_second: float32 [3, 256], replicated
- scalars: float32 [5], replicated
- grad_norm: float32 [1], replicated
The draws below stay inside these ranges and needn't reach their ends.
Inputs may be any that keep to these rules, and one draw needn't show every extreme that they name: Each index of dp holds its valid transitions in its first counts rows; some index is full. `a_w1_mom`: index 0 along the first dimension holds first moments, index 1 positive second moments. `a_w2_mom`: as for a_w1_mom. `a_head_mom`: as for a_w1_mom. `c_w1_mom`: as for a_w1_mom. `c_w2_mom`: as for a_w1_mom. `c_head_mom`: as for a_w1_mom. `bias2_mom`: as for a_w1_mom. `state`: the temperature's second moment and the std statistic are positive.
All inputs are finite; a program needn't handle non-finite values. No bound on the sum of `terminal` on one device may be relied on, other than what follows from the above.
Results may differ from the reference program's by a relative error of at most 0.0003.
The reference program's roundings to bfloat16 on the way count: a program that leaves them out, or rounds other values in their place, can miss the bound.
Values may be sent and summed in bfloat16 or wider, within the bound.
No kernel may reach another device: no remote copies, remote signals or barrier semaphores. Data moves between devices by JAX's collectives and lax.ppermute only.
A program may use at most 192 MiB of HBM per device.

```python
import math
import jax
import jax.numpy as jnp
from jax import lax

OBS = 376
ACT = 17
H = 256
B_DEV = 4096
TRANS = 65536
PARAMS = 505382
N_DP = 16


def moment_pair(key, shape):
    grad_size = 0.005 / math.sqrt(PARAMS)
    first_key, second_key = jax.random.split(key)
    first = jax.random.normal(first_key, shape, jnp.float32) * (0.111 * grad_size)
    spread = jnp.exp(jax.random.uniform(second_key, shape, jnp.float32, math.log(0.5), math.log(8.0)))
    second = spread * (0.001 / 0.999) * grad_size * grad_size
    return jnp.stack([first, second])


def draw_counts(key, part):
    value_key, full_key = jax.random.split(key)
    values = jax.random.randint(value_key, (N_DP,), B_DEV // 2, B_DEV + 1)
    full = jax.random.randint(full_key, (), 0, N_DP)
    return jnp.where(jnp.arange(N_DP) == full, B_DEV, values).astype(jnp.int32)


def draw_a_w1_mom(key, part):
    return moment_pair(key, (OBS + 1, H))


def draw_a_w2_mom(key, part):
    return moment_pair(key, (H, H))


def draw_a_head_mom(key, part):
    return moment_pair(key, (H + 1, 2 * ACT))


def draw_c_w1_mom(key, part):
    return moment_pair(key, (2, OBS + ACT + 1, H))


def draw_c_w2_mom(key, part):
    return moment_pair(key, (2, H, H))


def draw_c_head_mom(key, part):
    return moment_pair(key, (2, H + 1, 2))


def draw_bias2_mom(key, part):
    return moment_pair(key, (3, H))


def draw_state(key, part):
    lower = jnp.array([-3.0, -2.0, 1.0, 0.5], jnp.float32)
    upper = jnp.array([-1.0, 2.0, 4.0, 1.5], jnp.float32)
    return lower + (upper - lower) * jax.random.uniform(key, (4,), jnp.float32)


def plant(values, stream_key, least, largest):
    place = [jax.random.randint(jax.random.fold_in(stream_key, axis), (), 0, length) for axis, length in enumerate(values.shape)]
    main_axis = values.shape.index(max(values.shape))
    next_to = place[:main_axis] + [(place[main_axis] + 1) % values.shape[main_axis]] + place[main_axis + 1:]
    return values.at[tuple(place)].set(least).at[tuple(next_to)].set(largest)


def steps_of(own_key, dims, cuts, least, top_value):
    def one(axis_at, blocks):
        heights = jax.random.uniform(jax.random.fold_in(jax.random.fold_in(own_key, 6), axis_at), (blocks,), jnp.float32, least / len(cuts), top_value / len(cuts))
        return jnp.repeat(jnp.exp(heights), dims[axis_at] // blocks).reshape((-1,) + (1,) * (len(dims) - axis_at - 1))

    loudness = one(*cuts[0])
    for cut in cuts[1:]:
        loudness = loudness * one(*cut)
    return loudness


def gaussian(own_key, extent, deviation, bound, pieces=(), held_as=jnp.bfloat16):
    drawn = jax.random.normal(own_key, extent, jnp.float32) * deviation
    if len(pieces) > 0:
        drawn = steps_of(own_key, extent, pieces, -0.22, 0.18) * drawn
    return jnp.clip(drawn, min=-bound, max=bound).astype(held_as)


def setup_inputs(seed: int = 0) -> dict:
    arg_keys = jax.random.split(jax.random.key(seed), 29)
    obs = gaussian(arg_keys[0], (TRANS, OBS), 1.0, 6.0, ((0, 16),))
    action = jnp.clip(jax.random.uniform(arg_keys[1], (TRANS, ACT), jnp.float32, -0.94921875, 0.94921875) * steps_of(arg_keys[1], (TRANS, ACT), ((0, 16),), -0.4, 0.0), -0.94921875, 0.94921875).astype(jnp.bfloat16)
    next_obs = gaussian(arg_keys[2], (TRANS, OBS), 1.0, 6.0, ((0, 16),))
    reward = gaussian(arg_keys[3], (TRANS,), 1.0, 6.0, ((0, 16),), jnp.float32)
    terminal = plant((jax.random.randint(arg_keys[4], (TRANS,), 0, 10) < 1).astype(jnp.int32), jax.random.fold_in(arg_keys[4], 1), 0, 1)
    noise = gaussian(arg_keys[5], (TRANS, ACT), 1.0, 4.0, ((0, 16),), jnp.float32)
    next_noise = gaussian(arg_keys[6], (TRANS, ACT), 1.0, 4.0, ((0, 16),), jnp.float32)
    counts = draw_counts(jax.random.fold_in(arg_keys[28], 71), 0)
    step_count = jax.random.randint(arg_keys[8], (1,), 2, 22).astype(jnp.int32)
    a_w1 = gaussian(arg_keys[9], (OBS + 1, H), (OBS + 1) ** -0.5, 0.3125, ((1, 2),), jnp.float32)
    a_w2 = gaussian(arg_keys[10], (H, H), H ** -0.5, 0.375, ((0, 2),), jnp.float32)
    a_head = gaussian(arg_keys[11], (H + 1, 2 * ACT), H ** -0.5, 0.375, (), jnp.float32)
    c_w1 = gaussian(arg_keys[12], (2, OBS + ACT + 1, H), (OBS + ACT + 1) ** -0.5, 0.3125, ((2, 2),), jnp.float32)
    c_w2 = gaussian(arg_keys[13], (2, H, H), H ** -0.5, 0.375, ((1, 2),), jnp.float32)
    c_head = gaussian(arg_keys[14], (2, H + 1, 2), H ** -0.5, 0.375, (), jnp.float32)
    bias2 = gaussian(arg_keys[15], (3, H), 0.3, 1.5, (), jnp.float32)
    tc_w1 = gaussian(arg_keys[16], (2, OBS + ACT + 1, H), (OBS + ACT + 1) ** -0.5, 0.3125, ((2, 2),), jnp.float32)
    tc_w2 = gaussian(arg_keys[17], (2, H, H), H ** -0.5, 0.375, ((1, 2),), jnp.float32)
    tc_head = gaussian(arg_keys[18], (2, H + 1, 2), H ** -0.5, 0.375, (), jnp.float32)
    tc_bias2 = gaussian(arg_keys[19], (2, H), 0.3, 1.5, (), jnp.float32)
    a_w1_mom = draw_a_w1_mom(jax.random.fold_in(arg_keys[28], 71), 0)
    a_w2_mom = draw_a_w2_mom(jax.random.fold_in(arg_keys[28], 71), 0)
    a_head_mom = draw_a_head_mom(jax.random.fold_in(arg_keys[28], 71), 0)
    c_w1_mom = draw_c_w1_mom(jax.random.fold_in(arg_keys[28], 71), 0)
    c_w2_mom = draw_c_w2_mom(jax.random.fold_in(arg_keys[28], 71), 0)
    c_head_mom = draw_c_head_mom(jax.random.fold_in(arg_keys[28], 71), 0)
    bias2_mom = draw_bias2_mom(jax.random.fold_in(arg_keys[28], 71), 0)
    state = draw_state(jax.random.fold_in(arg_keys[28], 71), 0)
    return dict(obs=obs, action=action, next_obs=next_obs, reward=reward, terminal=terminal, noise=noise, next_noise=next_noise, counts=counts, step_count=step_count, a_w1=a_w1, a_w2=a_w2, a_head=a_head, c_w1=c_w1, c_w2=c_w2, c_head=c_head, bias2=bias2, tc_w1=tc_w1, tc_w2=tc_w2, tc_head=tc_head, tc_bias2=tc_bias2, a_w1_mom=a_w1_mom, a_w2_mom=a_w2_mom, a_head_mom=a_head_mom, c_w1_mom=c_w1_mom, c_w2_mom=c_w2_mom, c_head_mom=c_head_mom, bias2_mom=bias2_mom, state=state)


GAMMA = 0.99
RHO = 0.005
TAU_STAT = 0.1
CLIP = 0.005
RATE = 0.05
BETA_ONE = 0.9
BETA_TWO = 0.999
ADAM_EPS = 1e-08
DECAY = 0.01
HALF_LOG_TAU = 0.5 * math.log(2.0 * math.pi)
LOG_TWO = math.log(2.0)
HIGH = lax.Precision.HIGHEST

@jax.custom_vjp
def low(v):
    return lax.optimization_barrier(v.astype(jnp.bfloat16)).astype(jnp.float32)

@jax.custom_vjp
def low_back(v):
    return v

def low_keep(v):
    return (low(v), None)

def low_pass(kept, grad):
    return (grad,)

def back_keep(v):
    return (v, None)

def back_low(kept, grad):
    return (low(grad),)
low.defvjp(low_keep, low_pass)
low_back.defvjp(back_keep, back_low)

def with_ones(parts, copies):
    ones = jnp.ones((parts[0].shape[0], 1), jnp.float32)
    joined = jnp.concatenate(parts + [ones], axis=1)
    return jnp.broadcast_to(joined[None], (copies,) + joined.shape)

def network(inputs, w_first, w_second, b_second, w_head):
    z_first = low_back(jnp.einsum('crk,ckh->crh', inputs, low(w_first), precision=HIGH))
    h_first = low(jax.nn.gelu(z_first))
    z_second = low_back(jnp.einsum('crh,chg->crg', h_first, low(w_second), precision=HIGH))
    h_second = low(jax.nn.gelu(z_second + b_second[:, None, :]))
    ones = jnp.ones(h_second.shape[:2] + (1,), jnp.float32)
    h_aug = jnp.concatenate([h_second, ones], axis=2)
    return low_back(jnp.einsum('crg,cgo->cro', h_aug, low(w_head), precision=HIGH))

def policy_post(out, noise):
    mean = out[:, :ACT]
    log_std = jnp.tanh(out[:, ACT:]) - 1.0
    u_pre = mean + jnp.exp(log_std) * noise
    act = jnp.tanh(u_pre)
    terms = -0.5 * noise * noise - log_std - HALF_LOG_TAU - 2.0 * (LOG_TWO - u_pre - jax.nn.softplus(-2.0 * u_pre))
    return (act, lax.optimization_barrier(jnp.sum(terms, axis=1)))

def critic_terms(out, target, weight, valid):
    q_mean = out[..., 0]
    log_sigma = jnp.tanh(out[..., 1])
    sigma = jnp.exp(log_sigma)
    error = target[None] - q_mean
    terms = weight * (error * error / (2.0 * sigma * sigma) + log_sigma)
    return (jnp.sum(valid[None] * terms), jnp.sum(valid[None] * sigma))

def adam_step(weight, moments, grad, first_fix, second_fix, decay):
    first = BETA_ONE * moments[0] + (1.0 - BETA_ONE) * grad
    second = BETA_TWO * moments[1] + (1.0 - BETA_TWO) * grad * grad
    step = first / first_fix / (jnp.sqrt(second / second_fix) + ADAM_EPS)
    return (weight - RATE * (step + decay * weight), first, second)

def reference(obs, action, next_obs, reward, terminal, noise, next_noise, counts, step_count, a_w1, a_w2, a_head, c_w1, c_w2, c_head, bias2, tc_w1, tc_w2, tc_head, tc_bias2, a_w1_mom, a_w2_mom, a_head_mom, c_w1_mom, c_w2_mom, c_head_mom, bias2_mom, state):
    rows = obs.shape[0]
    row_ids = jnp.arange(rows, dtype=jnp.int32)
    valid = (row_ids % B_DEV < counts[row_ids // B_DEV]).astype(jnp.float32)
    count = jnp.sum(counts.astype(jnp.float32))
    alpha = jnp.exp(state[0])
    omega = state[3] * state[3]
    obs_f = obs.astype(jnp.float32)
    next_f = next_obs.astype(jnp.float32)
    action_f = action.astype(jnp.float32)
    out_next = network(with_ones([next_f], 1), a_w1[None], a_w2[None], bias2[0:1], a_head[None])[0]
    act_next, logp_next = policy_post(out_next, next_noise)
    q_target = network(with_ones([next_f, low(act_next)], 2), tc_w1, tc_w2, tc_bias2, tc_head)
    target = reward + GAMMA * (1.0 - terminal.astype(jnp.float32)) * (jnp.minimum(q_target[0, :, 0], q_target[1, :, 0]) - alpha * logp_next)
    next_sum = jnp.sum(valid * (logp_next - ACT))

    def objective(params):
        p_w1, p_w2, p_head, q_w1, q_w2, q_head, p_bias, log_alpha = params
        out_a = network(with_ones([obs_f], 1), p_w1[None], p_w2[None], p_bias[0:1], p_head[None])[0]
        act, logp = policy_post(out_a, noise)
        q_new = network(with_ones([obs_f, low(act)], 2), c_w1, c_w2, bias2[1:3], c_head)
        actor_sum = jnp.sum(valid * (alpha * logp - 0.5 * (q_new[0, :, 0] + q_new[1, :, 0])))
        q_data = network(with_ones([obs_f, action_f], 2), q_w1, q_w2, p_bias[1:3], q_head)
        critic_sum, sigma_sum = critic_terms(q_data, target, omega, valid)
        return (critic_sum + actor_sum - log_alpha * next_sum, sigma_sum)
    params = (a_w1, a_w2, a_head, c_w1, c_w2, c_head, bias2, state[0])
    total, pull, sigma_sum = jax.vjp(objective, params, has_aux=True)
    grads = [g / count for g in pull(jnp.float32(1.0))[0]]
    weight_grads = grads[:7]
    grad_norm = jnp.sqrt(sum((jnp.sum(g * g) for g in weight_grads)))
    clip = jnp.minimum(1.0, CLIP / (grad_norm + 1e-06))
    t_step = step_count[0].astype(jnp.float32)
    first_fix = 1.0 - jnp.power(BETA_ONE, t_step)
    second_fix = 1.0 - jnp.power(BETA_TWO, t_step)
    weights = [a_w1, a_w2, a_head, c_w1, c_w2, c_head, bias2]
    moments = [a_w1_mom, a_w2_mom, a_head_mom, c_w1_mom, c_w2_mom, c_head_mom, bias2_mom]
    results = []
    for weight, mom, grad in zip(weights, moments, weight_grads):
        results.append(adam_step(weight, mom, clip * grad, first_fix, second_fix, DECAY))
    tc_w1_new = (1.0 - RHO) * tc_w1 + RHO * results[3][0]
    tc_w2_new = (1.0 - RHO) * tc_w2 + RHO * results[4][0]
    tc_head_new = (1.0 - RHO) * tc_head + RHO * results[5][0]
    tc_bias2_new = (1.0 - RHO) * tc_bias2 + RHO * results[6][0][1:3]
    alpha_new, alpha_first, alpha_second = adam_step(state[0], state[1:3], grads[7], first_fix, second_fix, 0.0)
    stat_new = (1.0 - TAU_STAT) * state[3] + TAU_STAT * sigma_sum / (2.0 * count)
    scalars = jnp.stack([alpha_new, alpha_first, alpha_second, stat_new, total / count])
    return (results[0][0], results[0][1], results[0][2], results[1][0], results[1][1], results[1][2], results[2][0], results[2][1], results[2][2], jnp.concatenate([results[3][0], tc_w1_new]), results[3][1], results[3][2], jnp.concatenate([results[4][0], tc_w2_new]), results[4][1], results[4][2], jnp.concatenate([results[5][0], tc_head_new]), results[5][1], results[5][2], jnp.concatenate([results[6][0], tc_bias2_new]), results[6][1], results[6][2], scalars, grad_norm[None])
```

```python
import functools
import math

import jax
import jax.numpy as jnp
from jax import lax
from jax.experimental import pallas as pl
from jax.experimental.pallas import tpu as pltpu
from jax.sharding import PartitionSpec as P

OBS = 376
ACT = 17
H = 256
GAMMA = 0.99
RHO = 0.005
TAU_STAT = 0.1
CLIP = 0.005
RATE = 0.05
BETA_ONE = 0.9
BETA_TWO = 0.999
ADAM_EPS = 1e-08
DECAY = 0.01
HALF_LOG_TAU = 0.5 * math.log(2.0 * math.pi)
LOG_TWO = math.log(2.0)
GELU_A = math.sqrt(2.0 / math.pi)
GELU_B = GELU_A * 0.044715
F32 = jnp.float32
B16 = jnp.bfloat16

A_IN = OBS + 1
C_IN = OBS + ACT + 1
BIAS_ROW = OBS + ACT
K_PAD = 512
K_USE = 400
HALF = H // 2
VMEM = pltpu.VMEM
VMEM_LIMIT = 62 * 1024 * 1024

PACK_W2 = 5 * 4 * HALF
PACK_ACT = PACK_W2 + 5 * 2 * HALF
PACK_ROWS = PACK_ACT + 2 * 32

FLAT_CW1 = 0
FLAT_AW1 = 792
FLAT_AW2 = FLAT_AW1 + 384
FLAT_CW2 = FLAT_AW2 + H
FLAT_SMALL = FLAT_CW2 + 2 * H
FLAT_AHEAD = FLAT_SMALL
FLAT_CHEAD = FLAT_AHEAD + 80
FLAT_B2 = FLAT_CHEAD + 8
FLAT_SUMS = FLAT_B2 + 8
FLAT_ROWS = FLAT_SUMS + 8
LANE_C = 48
LANE_LOSS = 64
LANE_SIGMA = 72
LANE_NEXT = 80
LANE_COUNT = 88


def dot_nn(a, b):
    return lax.dot_general(a, b, (((1,), (0,)), ((), ())), preferred_element_type=F32)


def dot_nt(a, b):
    return lax.dot_general(a, b, (((1,), (1,)), ((), ())), preferred_element_type=F32)


def gelu_only(z):
    zz = z * z
    t = jnp.tanh(z * (GELU_A + GELU_B * zz))
    return z * (0.5 + 0.5 * t)


def gelu_both(z):
    zz = z * z
    s = 0.5 + 0.5 * jnp.tanh(z * (GELU_A + GELU_B * zz))
    value = z * s
    slope = s + value * (1.0 - s) * (2.0 * GELU_A + 6.0 * GELU_B * zz)
    return value, slope


def pack_kernel(a_w1, c_w1, t_w1, a_w2, c_w2, t_w2, out, wide):
    for net in range(5):
        wide[...] = jnp.zeros_like(wide)
        if net == 0:
            wide[0:OBS, :] = a_w1[0:OBS, :]
            wide[BIAS_ROW : BIAS_ROW + 1, :] = a_w1[OBS:A_IN, :]
        else:
            source = c_w1 if net < 3 else t_w1
            wide[0:C_IN, :] = source[:, (net - 1) % 2, :]
        for tile in range(4):
            base = (net * 4 + tile) * HALF
            out[base : base + HALF, :] = jnp.transpose(wide[tile * 128 : tile * 128 + 128, :]).astype(B16)
        if net in (1, 2):
            base = PACK_ACT + (net - 1) * 32
            rows = lax.broadcasted_iota(jnp.int32, (32, 128), 0)
            out[base : base + 32, :] = jnp.where(rows < ACT, wide[OBS : OBS + 32, :], 0.0).astype(B16)
        for part in range(2):
            base = PACK_W2 + (net * 2 + part) * HALF
            lanes = slice(part * 128, part * 128 + 128)
            if net == 0:
                block = a_w2[:, lanes]
            else:
                block = (c_w2 if net < 3 else t_w2)[(net - 1) % 2, :, lanes]
            out[base : base + HALF, :] = block.astype(B16)


def pack_weights(a_w1, c_w1, t_w1, a_w2, c_w2, t_w2):
    return pl.pallas_call(
        pack_kernel,
        out_shape=jax.ShapeDtypeStruct((PACK_ROWS, 128), B16),
        scratch_shapes=[VMEM((K_PAD, 128), F32)],
        name="pack",
    )(a_w1, c_w1, t_w1, a_w2, c_w2, t_w2)


def step_kernel(
    rows_tile,
    chunk_ids,
    n_own,
    count_ref,
    state_ref,
    obs_ref,
    next_ref,
    action_ref,
    noise_ref,
    next_noise_ref,
    reward_ref,
    terminal_ref,
    pack_own,
    pack_par,
    a_head_ref,
    c_head_ref,
    t_head_ref,
    bias2_ref,
    t_bias2_ref,
    *rest,
):
    own_outs = rest[:n_own]
    par_out = rest[n_own]
    (
        w1t, w2, w2t, w1a, wht_a, wh_a, wht_c, wh_c, hb, b2b,
        xn, xd, xq,
        z1, z1q, z2, z2q, zn, zt, h1n, h2n, h1, h2, h1q, h2q, h1t, h2t,
        g1, g1q, g2, g2q,
        dz1, dz2, dzq1, dzq2,
        acc1, acc2, acc_ha, acc_hc, acc_b, acc_s, flat,
    ) = rest[n_own + 1 :]
    step = pl.program_id(0)
    n_steps = pl.num_programs(0)
    t_index = lax.axis_index("tensor")
    rt = rows_tile
    lane_tiles = rt // 128

    @pl.when(step == 0)
    def _():
        for net in range(5):
            for side, pack in enumerate((pack_own, pack_par)):
                rows = slice(net * H + side * HALF, net * H + side * HALF + HALF)
                for tile in range(4):
                    base = (net * 4 + tile) * HALF
                    w1t[rows, tile * 128 : tile * 128 + 128] = pack[base : base + HALF, :]
                for part in range(2):
                    base = PACK_W2 + (net * 2 + part) * HALF
                    w2[rows, part * 128 : part * 128 + 128] = pack[base : base + HALF, :]
        for side, pack in enumerate((pack_own, pack_par)):
            w1a[:, side * HALF : side * HALF + HALF] = pack[PACK_ACT:PACK_ROWS, :]
        for net in range(5):
            w2t[net * H : net * H + H, :] = jnp.transpose(w2[net * H : net * H + H, :])
        wht_a[...] = jnp.zeros_like(wht_a)
        hb[...] = jnp.zeros_like(hb)
        for part in range(2):
            rows = a_head_ref[part * ACT : part * ACT + ACT, :].astype(B16)
            wht_a[part * 24 : part * 24 + ACT, :] = rows[:, 0:H].astype(F32)
            hb[part * 24 : part * 24 + ACT, :] = jnp.broadcast_to(rows[:, H : H + 1].astype(F32), (ACT, 128))
        wh_a[...] = jnp.transpose(wht_a[...]).astype(B16)
        wht_c[...] = jnp.zeros_like(wht_c)
        for net in range(4):
            head = (c_head_ref if net < 2 else t_head_ref)[net % 2].astype(B16).astype(F32)
            wht_c[net * 8 : net * 8 + 2, :] = head[:, 0:H]
            hb[48 + net * 8 : 48 + net * 8 + 2, :] = jnp.broadcast_to(head[:, H : H + 1], (2, 128))
        wh_c[...] = jnp.transpose(wht_c[...]).astype(B16)
        for net in range(5):
            bias = bias2_ref[net : net + 1, :] if net < 3 else t_bias2_ref[net - 3 : net - 2, :]
            b2b[net * H : net * H + H, :] = jnp.transpose(jnp.broadcast_to(bias, (128, H)))
        tail = lax.broadcasted_iota(jnp.int32, (K_PAD - OBS, rt), 0)
        ones = jnp.where(tail == ACT, 1.0, 0.0).astype(B16)
        xn[OBS:K_PAD, :] = ones
        xd[OBS:K_PAD, :] = ones
        xq[OBS:K_PAD, :] = ones
        acc1[...] = jnp.zeros_like(acc1)
        acc2[...] = jnp.zeros_like(acc2)
        acc_ha[...] = jnp.zeros_like(acc_ha)
        acc_hc[...] = jnp.zeros_like(acc_hc)
        acc_b[...] = jnp.zeros_like(acc_b)
        acc_s[...] = jnp.zeros_like(acc_s)

    def lanes_of(column, rows):
        return jnp.concatenate([column] * lane_tiles, axis=1)

    def lane_sum(value):
        total = value[:, 0:128]
        for tile in range(1, lane_tiles):
            total = total + value[:, tile * 128 : tile * 128 + 128]
        return total

    def act_rows(source, target, slope, rows, bias_base=None):
        for r in range(0, rows, 16):
            z = source[r : r + 16, :]
            if bias_base is not None:
                z = z + lanes_of(b2b[bias_base + r : bias_base + r + 16, :], 16)
            if slope is None:
                target[r : r + 16, :] = gelu_only(z).astype(B16)
            else:
                value, grad = gelu_both(z)
                target[r : r + 16, :] = value.astype(B16)
                slope[r : r + 16, :] = grad

    xn[0:OBS, :] = next_ref[...]
    xd[0:OBS, :] = obs_ref[...]
    xq[0:OBS, :] = obs_ref[...]
    xd[OBS : OBS + ACT, :] = action_ref[...]

    index = t_index * (n_steps * rt) + step * rt + lax.broadcasted_iota(jnp.int32, (1, rt), 1)
    valid = (index < count_ref[0]).astype(F32)
    alpha = jnp.exp(jnp.full((1, rt), state_ref[0], F32))
    omega = state_ref[3] * state_ref[3]

    zn[...] = dot_nn(w1t[0:H, :], xn[...])
    z1[...] = dot_nn(w1t[0 : 3 * H, :], xd[...])
    act_rows(zn, h1n, None, H)
    act_rows(z1, h1, g1, 3 * H)
    zn[...] = dot_nn(w2t[0:H, :], h1n[...])
    for net in range(3):
        rows = slice(net * H, net * H + H)
        z2[rows, :] = dot_nn(w2t[rows, :], h1[rows, :])
    act_rows(zn, h2n, None, H, 0)
    act_rows(z2, h2, g2, 3 * H, 0)

    wht_a16 = wht_a[...].astype(B16)
    hb_a = lanes_of(hb[0:48, :], 48)

    def policy(hidden, noise):
        out = dot_nn(wht_a16, hidden) + hb_a
        pad = jnp.zeros((24 - ACT, rt), F32)
        eps = jnp.concatenate([noise, pad], axis=0)
        tl = jnp.tanh(out[24:48])
        ls = tl - 1.0
        spread = jnp.exp(ls) * eps
        u = out[0:24] + spread
        act = jnp.tanh(u)
        soft = jnp.maximum(-2.0 * u, 0.0) + jnp.log(1.0 + jnp.exp(-jnp.abs(2.0 * u)))
        terms = -0.5 * eps * eps - ls - HALF_LOG_TAU - 2.0 * (LOG_TWO - u - soft)
        keep = lax.broadcasted_iota(jnp.int32, (24, rt), 0) < ACT
        logp = jnp.sum(jnp.where(keep, terms, 0.0), axis=0, keepdims=True)
        return act, logp, tl, spread

    act_next, logp_next, _, _ = policy(h2n[...], next_noise_ref[...])
    act_new, logp_new, tl_new, spread_new = policy(h2[0:H, :], noise_ref[...])
    xn[OBS : OBS + ACT, :] = act_next[0:ACT].astype(B16)
    xq[OBS : OBS + ACT, :] = act_new[0:ACT].astype(B16)

    zt[...] = dot_nn(w1t[3 * H : 5 * H, :], xn[...])
    z1q[...] = dot_nn(w1t[H : 3 * H, :], xq[...])
    act_rows(zt, h1t, None, 2 * H)
    act_rows(z1q, h1q, g1q, 2 * H)
    for net in range(2):
        rows = slice(net * H, net * H + H)
        zt[rows, :] = dot_nn(w2t[(3 + net) * H : (4 + net) * H, :], h1t[rows, :])
        z2q[rows, :] = dot_nn(w2t[(1 + net) * H : (2 + net) * H, :], h1q[rows, :])
    act_rows(zt, h2t, None, 2 * H, 3 * H)
    act_rows(z2q, h2q, g2q, 2 * H, H)

    wht_c16 = wht_c[...].astype(B16)

    def head(net, hidden):
        rows = slice(net * 8, net * 8 + 8)
        return dot_nn(wht_c16[rows], hidden) + lanes_of(hb[48 + net * 8 : 56 + net * 8, :], 8)

    out_t = [head(2 + net, h2t[net * H : net * H + H, :])[0:1] for net in range(2)]
    out_d = [head(net, h2[(1 + net) * H : (2 + net) * H, :]) for net in range(2)]
    out_q = [head(net, h2q[net * H : net * H + H, :])[0:1] for net in range(2)]
    alive = 1.0 - terminal_ref[...].astype(F32)
    target = reward_ref[...] + GAMMA * alive * (jnp.minimum(out_t[0], out_t[1]) - alpha * logp_next)

    loss_row = valid * (alpha * logp_new - 0.5 * (out_q[0] + out_q[1]))
    sigma_row = jnp.zeros((1, rt), F32)
    next_row = valid * (logp_next - ACT)
    d_heads = []
    for net in range(2):
        log_sigma = jnp.tanh(out_d[net][1:2])
        sigma = jnp.exp(log_sigma)
        error = target - out_d[net][0:1]
        inverse = 1.0 / (sigma * sigma)
        scaled = error * inverse
        square = error * scaled
        loss_row = loss_row + valid * (omega * (0.5 * square + log_sigma))
        sigma_row = sigma_row + valid * sigma
        d_q = -(omega * valid) * scaled
        d_s = (omega * valid) * (1.0 - square) * (1.0 - log_sigma * log_sigma)
        d_heads.append(jnp.concatenate([d_q, d_s, jnp.zeros((6, rt), F32)], axis=0).astype(B16))
    acc_s[64:65, :] += lane_sum(loss_row)
    acc_s[72:73, :] += lane_sum(sigma_row)
    acc_s[80:81, :] += lane_sum(next_row)

    for net in range(2):
        rows = slice((1 + net) * H, (2 + net) * H)
        acc_s[48 + net * 8 : 56 + net * 8, :] += lane_sum(d_heads[net].astype(F32))
        acc_hc[net * 8 : net * 8 + 8, :] += dot_nt(d_heads[net], h2[rows, :])
        z2[rows, :] = dot_nn(wh_c[:, net * 8 : net * 8 + 8], d_heads[net])
    d_new = -0.5 * valid

    def back_second(source, slope, target, rows, acc):
        for r in rows:
            d_pre = source[r : r + 16, :] * slope[r : r + 16, :]
            target[r : r + 16, :] = d_pre.astype(B16)
            acc_b[r : r + 16, :] += lane_sum(d_pre)

    def back_first(source, slope, target, first, last, shift=0):
        for r in range(first, last, 16):
            target[r : r + 16, :] = (source[r + shift : r + shift + 16, :] * slope[r : r + 16, :]).astype(B16)

    back_second(z2, g2, dz2, range(H, 3 * H, 16), acc_b)
    for net in range(2):
        for r in range(0, H, 16):
            column = wh_c[r : r + 16, net * 8 : net * 8 + 1].astype(F32)
            d_hidden = column * d_new
            base = net * H + r
            dzq2[base : base + 16, :] = (d_hidden * g2q[base : base + 16, :]).astype(B16)
    for net in range(2):
        rows = slice(net * H, net * H + H)
        rows_c = slice((1 + net) * H, (2 + net) * H)
        z1q[rows, :] = dot_nn(w2[rows_c, :], dzq2[rows, :])
        z1[rows_c, :] = dot_nn(w2[rows_c, :], dz2[rows_c, :])
    back_first(z1q, g1q, dzq1, 0, 2 * H)
    back_first(z1, g1, dz1, H, 3 * H)
    d_act = dot_nn(w1a[0:32, :], dzq1[0:H, :]) + dot_nn(w1a[32:64, :], dzq1[H : 2 * H, :])
    d_act = d_act[0:24]

    d_logp = alpha * valid
    d_u = d_act * (1.0 - act_new * act_new) + (2.0 * d_logp) * act_new
    d_ls = (d_u * spread_new - d_logp) * (1.0 - tl_new * tl_new)
    d_out = jnp.concatenate([d_u, d_ls], axis=0).astype(B16)
    acc_s[0:48, :] += lane_sum(d_out.astype(F32))
    acc_ha[...] += dot_nt(d_out, h2[0:H, :])
    z2[0:H, :] = dot_nn(wh_a[...], d_out)
    back_second(z2, g2, dz2, range(0, H, 16), acc_b)
    z1[0:H, :] = dot_nn(w2[0:H, :], dz2[0:H, :])
    back_first(z1, g1, dz1, 0, H)

    for net in range(3):
        rows = slice(net * H, net * H + H)
        acc2[rows, :] += dot_nt(h1[rows, :], dz2[rows, :])
    acc1[...] += dot_nt(xd[0:K_USE, :], dz1[...])

    @pl.when(step == n_steps - 1)
    def _():
        d_index = lax.axis_index("dp")
        flat[:, FLAT_SMALL:FLAT_ROWS, :] = jnp.zeros((2, FLAT_ROWS - FLAT_SMALL, 128), F32)
        flat[:, FLAT_AW1 - 8 : FLAT_AW1, :] = jnp.zeros((2, 8, 128), F32)
        flat[:, FLAT_AW2 - 8 : FLAT_AW2, :] = jnp.zeros((2, 8, 128), F32)
        sums = jnp.sum(jnp.transpose(acc_s[...]), axis=0, keepdims=True)
        lane = lax.broadcasted_iota(jnp.int32, (1, 128), 1)
        keep = (lane < ACT) | ((lane >= 24) & (lane < 24 + ACT)) | ((lane >= 48) & (lane < 50))
        keep = keep | ((lane >= 56) & (lane < 58)) | (lane == LANE_LOSS) | (lane == LANE_SIGMA) | (lane == LANE_NEXT)
        sums = jnp.where(keep, sums, 0.0)
        sums = jnp.where(lane == LANE_COUNT, 0.5 * count_ref[0].astype(F32), sums)
        for side in range(2):
            lanes = slice(side * HALF, side * HALF + HALF)
            for net in range(2):
                columns = slice((1 + net) * H + side * HALF, (1 + net) * H + side * HALF + HALF)
                flat[side, pl.ds(FLAT_CW1 + net, C_IN, stride=2), :] = acc1[0:C_IN, columns]
            flat[side, FLAT_AW1 : FLAT_AW1 + OBS, :] = acc1[0:OBS, lanes]
            flat[side, FLAT_AW1 + OBS : FLAT_AW1 + A_IN, :] = acc1[BIAS_ROW : BIAS_ROW + 1, lanes]
            for net in range(3):
                rows = slice(net * H + side * HALF, net * H + side * HALF + HALF)
                for part in range(2):
                    base = FLAT_AW2 + (net * 2 + part) * HALF
                    flat[side, base : base + HALF, :] = acc2[rows, part * 128 : part * 128 + 128]
            for part in range(2):
                cols = slice(part * 128, part * 128 + 128)
                base = FLAT_AHEAD + part * 40
                flat[side, base : base + ACT, :] = acc_ha[0:ACT, cols]
                flat[side, base + ACT : base + 2 * ACT, :] = acc_ha[24 : 24 + ACT, cols]
                for net in range(2):
                    base = FLAT_CHEAD + part * 4 + net * 2
                    flat[side, base : base + 2, :] = acc_hc[net * 8 : net * 8 + 2, cols]
            for net in range(3):
                for part in range(2):
                    rows = slice(net * H + part * 128, net * H + part * 128 + 128)
                    row = FLAT_B2 + part * 4 + net
                    flat[side, row : row + 1, :] = jnp.sum(jnp.transpose(acc_b[rows, :]), axis=0, keepdims=True)
            flat[side, FLAT_SUMS : FLAT_SUMS + 1, :] = sums
        size = FLAT_ROWS // len(chunk_ids)
        per = len(chunk_ids) // n_own
        for place, rel in enumerate(chunk_ids):
            start = pl.multiple_of(jnp.bitwise_xor(d_index, rel) * size, size)
            own_outs[place // per][(place % per) * size : (place % per) * size + size, :] = flat[0, pl.ds(start, size), :]
            par_out[place * size : place * size + size, :] = flat[1, pl.ds(start, size), :]


def run_step(groups, arrays, pack_own, pack_par, small, count, state):
    obs, next_obs, action, noise, next_noise, reward, terminal = arrays
    rows = obs.shape[1] // groups["tensor"]
    rt = min(512, rows)
    steps = rows // rt
    chunk_ids, n_own = groups["order"], groups["first"]

    def tile(height):
        return pl.BlockSpec((height, rt), lambda i: (0, lax.axis_index("tensor") * steps + i))

    whole = pl.BlockSpec(memory_space=VMEM)
    smem = pl.BlockSpec(memory_space=pltpu.SMEM)
    scratch = [
        VMEM((5 * H, K_PAD), B16), VMEM((5 * H, H), B16), VMEM((5 * H, H), B16), VMEM((64, H), B16),
        VMEM((48, H), F32), VMEM((H, 48), B16), VMEM((32, H), F32), VMEM((H, 32), B16),
        VMEM((80, 128), F32), VMEM((5 * H, 128), F32),
        VMEM((K_PAD, rt), B16), VMEM((K_PAD, rt), B16), VMEM((K_PAD, rt), B16),
        VMEM((3 * H, rt), F32), VMEM((2 * H, rt), F32), VMEM((3 * H, rt), F32), VMEM((2 * H, rt), F32),
        VMEM((H, rt), F32), VMEM((2 * H, rt), F32),
        VMEM((H, rt), B16), VMEM((H, rt), B16), VMEM((3 * H, rt), B16), VMEM((3 * H, rt), B16),
        VMEM((2 * H, rt), B16), VMEM((2 * H, rt), B16), VMEM((2 * H, rt), B16), VMEM((2 * H, rt), B16),
        VMEM((3 * H, rt), F32), VMEM((2 * H, rt), F32), VMEM((3 * H, rt), F32), VMEM((2 * H, rt), F32),
        VMEM((3 * H, rt), B16), VMEM((3 * H, rt), B16), VMEM((2 * H, rt), B16), VMEM((2 * H, rt), B16),
        VMEM((K_USE, 3 * H), F32), VMEM((3 * H, H), F32), VMEM((48, H), F32), VMEM((16, H), F32),
        VMEM((3 * H, 128), F32), VMEM((128, 128), F32), VMEM((2, FLAT_ROWS, 128), F32),
    ]
    outs = [jax.ShapeDtypeStruct((FLAT_ROWS // n_own, 128), F32)] * n_own + [jax.ShapeDtypeStruct((FLAT_ROWS, 128), F32)]
    return pl.pallas_call(
        functools.partial(step_kernel, rt, chunk_ids, n_own),
        grid=(steps,),
        in_specs=[smem, smem, tile(OBS), tile(OBS), tile(ACT), tile(ACT), tile(ACT), tile(1), tile(1)] + [whole] * 7,
        out_specs=[whole] * (n_own + 1),
        out_shape=outs,
        scratch_shapes=scratch,
        compiler_params=pltpu.CompilerParams(vmem_limit_bytes=VMEM_LIMIT),
        name="step",
    )(count, state, obs, next_obs, action, noise, next_noise, reward, terminal, pack_own, pack_par, *small)


def last_sum_kernel(size, n_in, *refs):
    total = refs[0][...]
    for ref in refs[1:n_in]:
        total = total + ref[...]
    out, square = refs[n_in:]
    out[...] = total
    row = lax.axis_index("dp") * size + lax.broadcasted_iota(jnp.int32, (size, 128), 0)
    lane = lax.broadcasted_iota(jnp.int32, (size, 128), 1)
    weight = jnp.where(row < FLAT_SMALL, 1.0, 0.5)
    weight = jnp.where((row >= FLAT_SUMS) & (lane >= LANE_LOSS), 0.0, weight)
    squares = total * total * weight
    part = squares[0:8]
    for r in range(8, size, 8):
        part = part + squares[r : r + 8]
    square[...] = part


def last_sum(values, size):
    return pl.pallas_call(
        functools.partial(last_sum_kernel, size, len(values)),
        out_shape=[jax.ShapeDtypeStruct((size, 128), F32), jax.ShapeDtypeStruct((8, 128), F32)],
        name="lastsum",
    )(*values)


def one_minus_power(gap, exponent):
    total = jnp.float32(0.0)
    for bit in range(30, -1, -1):
        total = total * (2.0 - total)
        total = jnp.where((exponent >> bit) & 1 == 1, total + gap * (1.0 - total), total)
    return total


def update_kernel(order, n_parts, sizes, *refs):
    parts = refs[:n_parts]
    (
        step_ref, state_ref,
        a_w1, a_w1_m, a_w2, a_w2_m, a_head, a_head_m,
        c_w1, c_w1_m, c_w2, c_w2_m, c_head, c_head_m, bias2, bias2_m,
        t_w1, t_w2, t_head, t_bias2,
        o_a_w1, o_a_w1_f, o_a_w1_s, o_a_w2, o_a_w2_f, o_a_w2_s, o_a_head, o_a_head_f, o_a_head_s,
        o_c_w1, o_c_w1_f, o_c_w1_s, o_c_w2, o_c_w2_f, o_c_w2_s, o_c_head, o_c_head_f, o_c_head_s,
        o_bias2, o_bias2_f, o_bias2_s, o_scalars, o_norm,
        flat,
    ) = refs[n_parts:]
    size, stride = sizes
    d_index = lax.axis_index("dp")
    per = len(order) // n_parts
    square = jnp.zeros((8, 128), F32)
    for place, rel in enumerate(order):
        start = pl.multiple_of(jnp.bitwise_xor(d_index, rel) * size, size)
        base = (place % per) * stride
        flat[pl.ds(start, size), :] = parts[place // per][base : base + size, :]
        square = square + parts[place // per][base + size : base + size + 8, :]
    sums = flat[FLAT_SUMS : FLAT_SUMS + 1, :]
    lane = lax.broadcasted_iota(jnp.int32, (1, 128), 1)

    def pick(index):
        return jnp.sum(jnp.where(lane == index, sums, 0.0), axis=1, keepdims=True)

    loss_sum, sigma_sum, next_sum, count = (pick(i) for i in (LANE_LOSS, LANE_SIGMA, LANE_NEXT, LANE_COUNT))
    inverse = 1.0 / count
    total = jnp.sum(jnp.sum(square, axis=0, keepdims=True), axis=1, keepdims=True)
    norm = jnp.sqrt(total) * inverse
    clip = jnp.minimum(1.0, CLIP / (norm + 1e-06))
    scale = clip * inverse
    t = step_ref[0]
    first_fix = one_minus_power(jnp.float32(0.1), t)
    second_fix = one_minus_power(jnp.float32(0.001), t)
    unfix_one = 1.0 / jnp.full((1, 1), first_fix, F32)
    unfix_two = 1.0 / jnp.full((1, 1), second_fix, F32)

    def adam(weight, first, second, grad, decay=DECAY):
        first = BETA_ONE * first + (1.0 - BETA_ONE) * grad
        second = BETA_TWO * second + (1.0 - BETA_TWO) * (grad * grad)
        step = first * unfix_one / (jnp.sqrt(second * unfix_two) + ADAM_EPS)
        if decay:
            step = step + decay * weight
        return weight - RATE * step, first, second

    def polyak(target, new):
        return (1.0 - RHO) * target + RHO * new

    new, first, second = adam(a_w1[...], a_w1_m[:, 0, :], a_w1_m[:, 1, :], flat[FLAT_AW1 : FLAT_AW1 + A_IN, :] * scale)
    o_a_w1[...] = new
    o_a_w1_f[...] = first
    o_a_w1_s[...] = second
    for net in range(3):
        for part in range(2):
            lanes = slice(part * 128, part * 128 + 128)
            base = FLAT_AW2 + (net * 2 + part) * HALF
            grad = flat[base : base + HALF, :] * scale
            if net == 0:
                new, first, second = adam(a_w2[:, lanes], a_w2_m[0, :, lanes], a_w2_m[1, :, lanes], grad)
                o_a_w2[:, lanes] = new
                o_a_w2_f[:, lanes] = first
                o_a_w2_s[:, lanes] = second
            else:
                c = net - 1
                new, first, second = adam(c_w2[c, :, lanes], c_w2_m[0, c, :, lanes], c_w2_m[1, c, :, lanes], grad)
                o_c_w2[c, :, lanes] = new
                o_c_w2[2 + c, :, lanes] = polyak(t_w2[c, :, lanes], new)
                o_c_w2_f[c, :, lanes] = first
                o_c_w2_s[c, :, lanes] = second
    for c in range(2):
        grad = flat[pl.ds(FLAT_CW1 + c, C_IN, stride=2), :] * scale
        new, first, second = adam(c_w1[:, c, :], c_w1_m[0, :, c, :], c_w1_m[1, :, c, :], grad)
        o_c_w1[:, c, :] = new
        o_c_w1[:, 2 + c, :] = polyak(t_w1[:, c, :], new)
        o_c_w1_f[:, c, :] = first
        o_c_w1_s[:, c, :] = second
    columns = jnp.transpose(jnp.broadcast_to(sums, (128, 128)))
    bias_a = jnp.concatenate([columns[0:ACT, 0:1], columns[24 : 24 + ACT, 0:1]], axis=0)
    grad = jnp.concatenate(
        [flat[FLAT_AHEAD : FLAT_AHEAD + 2 * ACT, :], flat[FLAT_AHEAD + 40 : FLAT_AHEAD + 40 + 2 * ACT, :], bias_a], axis=1
    )
    new, first, second = adam(a_head[...], a_head_m[:, 0, :], a_head_m[:, 1, :], grad * scale)
    o_a_head[...] = new
    o_a_head_f[...] = first
    o_a_head_s[...] = second
    for c in range(2):
        rows = slice(FLAT_CHEAD + c * 2, FLAT_CHEAD + c * 2 + 2)
        rows_b = slice(FLAT_CHEAD + 4 + c * 2, FLAT_CHEAD + 6 + c * 2)
        bias_c = columns[LANE_C + 8 * c : LANE_C + 8 * c + 2, 0:1]
        grad = jnp.concatenate([flat[rows, :], flat[rows_b, :], bias_c], axis=1) * scale
        new, first, second = adam(c_head[c], c_head_m[0, c], c_head_m[1, c], grad)
        o_c_head[c] = new
        o_c_head[2 + c] = polyak(t_head[c], new)
        o_c_head_f[c] = first
        o_c_head_s[c] = second
    grad = jnp.concatenate([flat[FLAT_B2 : FLAT_B2 + 3, :], flat[FLAT_B2 + 4 : FLAT_B2 + 7, :]], axis=1) * scale
    new, first, second = adam(bias2[...], bias2_m[:, 0, :], bias2_m[:, 1, :], grad)
    o_bias2[0:3, :] = new
    o_bias2[3:5, :] = polyak(t_bias2[...], new[1:3])
    o_bias2_f[...] = first
    o_bias2_s[...] = second
    log_alpha = jnp.full((1, 1), state_ref[0], F32)
    g_alpha = -next_sum
    new, first, second = adam(
        log_alpha, jnp.full((1, 1), state_ref[1], F32), jnp.full((1, 1), state_ref[2], F32), g_alpha * inverse, 0.0
    )
    stat = (1.0 - TAU_STAT) * state_ref[3] + TAU_STAT * sigma_sum / (2.0 * count)
    loss = (loss_sum + log_alpha * g_alpha) * inverse
    for place, value in enumerate((new, first, second, stat, loss)):
        o_scalars[place] = value[0, 0]
    o_norm[0] = norm[0, 0]


def kernel_view(value, order):
    return jnp.transpose(value, order)


def shards(
    groups, obs, action, next_obs, reward, terminal, noise, next_noise, counts, step_count,
    a_w1, a_w2, a_head, c_w1, c_w2, c_head, bias2, tc_w1, tc_w2, tc_head, tc_bias2,
    a_w1_mom, a_w2_mom, a_head_mom, c_w1_mom, c_w2_mom, c_head_mom, bias2_mom, state,
):
    n_dp = groups["dp"]
    swap = [(0, 1), (1, 0)]

    def partner(value):
        return lax.ppermute(value, "tensor", swap)

    def across(value, mask):
        return lax.ppermute(value, "dp", [(i, i ^ mask) for i in range(n_dp)])

    tr = jnp.transpose
    c_w1v, tc_w1v = tr(c_w1, (1, 0, 2)), tr(tc_w1, (1, 0, 2))
    a_headv, c_headv, tc_headv = tr(a_head), tr(c_head, (0, 2, 1)), tr(tc_head, (0, 2, 1))
    pack = pack_weights(a_w1, c_w1v, tc_w1v, a_w2, c_w2, tc_w2)
    pack_par = partner(pack)
    arrays = (
        tr(obs), tr(next_obs), tr(action), tr(noise), tr(next_noise), reward.reshape(1, -1), terminal.reshape(1, -1),
    )
    small = (a_headv, c_headv, tc_headv, bias2, tc_bias2)
    outs = run_step(groups, arrays, pack, pack_par, small, counts, state)
    own, par = outs[:-1], outs[-1]
    received = partner(par)
    size = FLAT_ROWS // len(own)
    values = [item + received[i * size : i * size + size] for i, item in enumerate(own)]

    phases = groups["phases"]
    for number, (shift, width) in enumerate(phases):
        ways = 1 << width
        got = [values[0]] + [across(values[k], k << shift) for k in range(1, ways)]
        if number < len(phases) - 1:
            following = 1 << phases[number + 1][1]
            size = got[0].shape[0] // following
            values = [sum(item[j * size : j * size + size] for item in got) for j in range(following)]
        else:
            size = got[0].shape[0]
            chunk, square = last_sum(got, size)
    square = square + partner(square)
    block = jnp.concatenate([chunk, square])
    for number, (shift, width) in reversed(list(enumerate(phases))):
        ways = 1 << width
        got = [block] + [across(block, k << shift) for k in range(1, ways)]
        if number:
            block = jnp.concatenate(got)
    parts = got

    sds = jax.ShapeDtypeStruct
    shapes = [
        (A_IN, HALF)] * 3 + [(HALF, H)] * 3 + [(2 * ACT, H + 1)] * 3 + [
        (C_IN, 4, HALF), (C_IN, 2, HALF), (C_IN, 2, HALF),
        (4, HALF, H), (2, HALF, H), (2, HALF, H),
        (4, 2, H + 1), (2, 2, H + 1), (2, 2, H + 1),
        (5, H), (3, H), (3, H), (5,), (1,),
    ]
    whole = pl.BlockSpec(memory_space=VMEM)
    smem = pl.BlockSpec(memory_space=pltpu.SMEM)
    res = pl.pallas_call(
        functools.partial(update_kernel, groups["order"], len(parts), (size, size + 8)),
        in_specs=[whole] * len(parts) + [smem, smem] + [whole] * 18,
        out_specs=[whole] * 21 + [smem, smem],
        out_shape=[sds(s, F32) for s in shapes],
        scratch_shapes=[VMEM((FLAT_ROWS, 128), F32)],
        compiler_params=pltpu.CompilerParams(vmem_limit_bytes=VMEM_LIMIT),
        name="update",
    )(
        *parts, step_count, state,
        a_w1, tr(a_w1_mom, (1, 0, 2)), a_w2, a_w2_mom, a_headv, tr(a_head_mom, (2, 0, 1)),
        c_w1v, tr(c_w1_mom, (0, 2, 1, 3)), c_w2, c_w2_mom, c_headv, tr(c_head_mom, (0, 1, 3, 2)),
        bias2, tr(bias2_mom, (1, 0, 2)), tc_w1v, tc_w2, tc_headv, tc_bias2,
    )
    res = list(res)
    for place in (6, 7, 8):
        res[place] = tr(res[place])
    for place in (9, 10, 11):
        res[place] = tr(res[place], (1, 0, 2))
    for place in (15, 16, 17):
        res[place] = tr(res[place], (0, 2, 1))
    return tuple(res)


def plan(mesh):
    n_dp = mesh.shape["dp"]
    bits = n_dp.bit_length() - 1
    assert n_dp == 1 << bits and mesh.shape["tensor"] == 2
    phases = []
    low = 0
    while low < bits:
        width = min(2, bits - low)
        phases.append((low, width))
        low += width
    order = [0]
    for shift, width in phases:
        order = [rel | (k << shift) for rel in order for k in range(1 << width)]
    return {
        "dp": n_dp, "tensor": mesh.shape["tensor"], "phases": phases, "order": tuple(order), "first": 1 << phases[0][1],
    }


def solution(mesh):
    in_specs = (
        P("dp", None), P("dp", None), P("dp", None), P("dp"), P("dp"), P("dp", None), P("dp", None), P("dp"), P(),
        P(None, "tensor"), P("tensor", None), P(), P(None, None, "tensor"), P(None, "tensor", None), P(), P(),
        P(None, None, "tensor"), P(None, "tensor", None), P(), P(),
        P(None, None, "tensor"), P(None, "tensor", None), P(), P(None, None, None, "tensor"),
        P(None, None, "tensor", None), P(), P(), P(),
    )
    out_specs = (
        P(None, "tensor"), P(None, "tensor"), P(None, "tensor"),
        P("tensor", None), P("tensor", None), P("tensor", None),
        P(), P(), P(),
        P(None, None, "tensor"), P(None, None, "tensor"), P(None, None, "tensor"),
        P(None, "tensor", None), P(None, "tensor", None), P(None, "tensor", None),
        P(), P(), P(), P(), P(), P(), P(), P(),
    )
    return jax.shard_map(
        functools.partial(shards, plan(mesh)), mesh=mesh, in_specs=in_specs, out_specs=out_specs, check_vma=False
    )
```

```python
import functools
import math

import jax
import jax.numpy as jnp
from jax import lax
from jax.experimental import pallas as pl
from jax.experimental.pallas import tpu as pltpu
from jax.sharding import PartitionSpec as P

OBS = 376
ACT = 17
H = 256
GAMMA = 0.99
RHO = 0.005
TAU_STAT = 0.1
CLIP = 0.005
RATE = 0.05
BETA_ONE = 0.9
BETA_TWO = 0.999
ADAM_EPS = 1e-08
DECAY = 0.01
HALF_LOG_TAU = 0.5 * math.log(2.0 * math.pi)
LOG_TWO = math.log(2.0)
GELU_A = math.sqrt(2.0 / math.pi)
GELU_B = GELU_A * 0.044715
F32 = jnp.float32
B16 = jnp.bfloat16

A_IN = OBS + 1
C_IN = OBS + ACT + 1
BIAS_ROW = OBS + ACT
K_PAD = 512
K_USE = 400
HALF = H // 2
VMEM = pltpu.VMEM
STEP_VMEM = 50 * 1024 * 1024
UPDATE_VMEM = 24 * 1024 * 1024
SMALL_VMEM = 8 * 1024 * 1024

PACK_W2 = 5 * 4 * HALF
PACK_ACT = PACK_W2 + 5 * 2 * HALF
PACK_ROWS = PACK_ACT + 2 * 32

FLAT_CW1 = 0
FLAT_AW1 = 792
FLAT_AW2 = FLAT_AW1 + 384
FLAT_CW2 = FLAT_AW2 + H
FLAT_SMALL = FLAT_CW2 + 2 * H
FLAT_AHEAD = FLAT_SMALL
FLAT_CHEAD = FLAT_AHEAD + 80
FLAT_B2 = FLAT_CHEAD + 8
FLAT_SUMS = FLAT_B2 + 8
FLAT_ROWS = FLAT_SUMS + 8
LANE_C = 48
LANE_LOSS = 64
LANE_SIGMA = 72
LANE_NEXT = 80
LANE_COUNT = 88


def dot_nn(a, b):
    return lax.dot_general(a, b, (((1,), (0,)), ((), ())), preferred_element_type=F32)


def dot_nt(a, b):
    return lax.dot_general(a, b, (((1,), (1,)), ((), ())), preferred_element_type=F32)


def gelu_only(y):
    t = jnp.tanh(y * (2.0 * GELU_A + (8.0 * GELU_B) * (y * y)))
    return y * (1.0 + t)


def gelu_both(y):
    w = y * y
    t = jnp.tanh(y * (2.0 * GELU_A + (8.0 * GELU_B) * w))
    e = 1.0 + t
    value = y * e
    return value, e + (value * (1.0 - t)) * (2.0 * GELU_A + (24.0 * GELU_B) * w)


def own_chunk(orders):
    d_index = lax.axis_index("dp")
    found = []
    for order in orders:
        number = jnp.int32(0)
        for place, bit in enumerate(order):
            number = number | (((d_index >> bit) & 1) << place)
        found.append(number)
    return jnp.where(lax.axis_index("tensor") == 0, found[0], found[1])


def pack_kernel(a_w1, c_w1, t_w1, a_w2, c_w2, t_w2, out, wide):
    for net in range(5):
        wide[...] = jnp.zeros_like(wide)
        if net == 0:
            wide[0:OBS, :] = a_w1[0:OBS, :]
            wide[BIAS_ROW : BIAS_ROW + 1, :] = a_w1[OBS:A_IN, :]
        else:
            source = c_w1 if net < 3 else t_w1
            wide[0:C_IN, :] = source.reshape(2 * C_IN, 128)[pl.ds((net - 1) % 2, C_IN, stride=2), :]
        for tile in range(4):
            base = (net * 4 + tile) * HALF
            out[base : base + HALF, :] = jnp.transpose(0.5 * wide[tile * 128 : tile * 128 + 128, :]).astype(B16)
        if net in (1, 2):
            base = PACK_ACT + (net - 1) * 32
            rows = lax.broadcasted_iota(jnp.int32, (32, 128), 0)
            out[base : base + 32, :] = jnp.where(rows < ACT, wide[OBS : OBS + 32, :], 0.0).astype(B16)
        for part in range(2):
            base = PACK_W2 + (net * 2 + part) * HALF
            lanes = slice(part * 128, part * 128 + 128)
            if net == 0:
                block = a_w2[:, lanes]
            else:
                block = (c_w2 if net < 3 else t_w2)[(net - 1) % 2, :, lanes]
            out[base : base + HALF, :] = (0.5 * block).astype(B16)


def in_hbm(*values):
    return [pltpu.with_memory_space_constraint(value, pltpu.HBM) for value in values]


def pack_weights(a_w1, c_w1, t_w1, a_w2, c_w2, t_w2):
    return pl.pallas_call(
        pack_kernel,
        out_shape=jax.ShapeDtypeStruct((PACK_ROWS, 128), B16),
        scratch_shapes=[VMEM((K_PAD, 128), F32)],
        compiler_params=pltpu.CompilerParams(vmem_limit_bytes=SMALL_VMEM),
        name="pack",
    )(*in_hbm(a_w1, c_w1, t_w1, a_w2, c_w2, t_w2))


def step_kernel(
    rows_tile,
    subs,
    offset,
    order,
    orders,
    n_own,
    count_ref,
    state_ref,
    obs_ref,
    next_ref,
    action_ref,
    noise_ref,
    next_noise_ref,
    reward_ref,
    terminal_ref,
    pack_own,
    pack_par,
    a_head_ref,
    c_head_ref,
    t_head_ref,
    bias2_ref,
    t_bias2_ref,
    *rest,
):
    own_outs = rest[:n_own]
    par_out = rest[n_own]
    (
        w1t, w2, w2t, w1a, wht_a, wh_a, wht_c, wh_c, hb, b2b, wqb,
        xn_all, xd_all, xq_all,
        z1_all, z1q_all, z2_all, z2q_all, zn_all, zt_all,
        h1n_all, h2n_all, h1_all, h2_all, h1q_all, h2q_all, h1t_all, h2t_all,
        g1_all, g1q_all, g2_all, dz1_all, dz2_all, dzq1_all, dzq2_all,
        acc1, acc2, acc_ha, acc_hc, acc_b, acc_s, flat,
    ) = rest[n_own + 1 :]
    step = pl.program_id(0)
    n_steps = pl.num_programs(0)
    t_index = lax.axis_index("tensor")
    rt = rows_tile
    lane_tiles = rt // 128

    @pl.when(step == 0)
    def _():
        for net in range(5):
            for side, pack in enumerate((pack_own, pack_par)):
                rows = slice(net * H + side * HALF, net * H + side * HALF + HALF)
                for tile in range(4):
                    base = (net * 4 + tile) * HALF
                    w1t[rows, tile * 128 : tile * 128 + 128] = pack[base : base + HALF, :]
                for part in range(2):
                    base = PACK_W2 + (net * 2 + part) * HALF
                    w2[rows, part * 128 : part * 128 + 128] = pack[base : base + HALF, :]
        for side, pack in enumerate((pack_own, pack_par)):
            w1a[:, side * HALF : side * HALF + HALF] = pack[PACK_ACT:PACK_ROWS, :]
        for net in range(5):
            w2t[net * H : net * H + H, :] = jnp.transpose(w2[net * H : net * H + H, :])
        wht_a[...] = jnp.zeros_like(wht_a)
        hb[...] = jnp.zeros_like(hb)
        for part in range(2):
            rows = a_head_ref[part * ACT : part * ACT + ACT, :].astype(B16)
            wht_a[part * 24 : part * 24 + ACT, :] = rows[:, 0:H].astype(F32)
            hb[part * 24 : part * 24 + ACT, :] = jnp.broadcast_to(rows[:, H : H + 1].astype(F32), (ACT, 128))
        wh_a[...] = jnp.transpose(0.5 * wht_a[...]).astype(B16)
        wht_c[...] = jnp.zeros_like(wht_c)
        for net in range(4):
            head = (c_head_ref if net < 2 else t_head_ref)[net % 2].astype(B16).astype(F32)
            wht_c[net * 8 : net * 8 + 2, :] = head[:, 0:H]
            hb[48 + net * 8 : 48 + net * 8 + 2, :] = jnp.broadcast_to(head[:, H : H + 1], (2, 128))
        wh_c[...] = jnp.transpose(0.5 * wht_c[...]).astype(B16)
        for net in range(2):
            row = 0.5 * wht_c[net * 8 : net * 8 + 1, :]
            wqb[net * H : net * H + H, :] = jnp.transpose(jnp.broadcast_to(row, (128, H)))
        for net in range(5):
            bias = bias2_ref[net : net + 1, :] if net < 3 else t_bias2_ref[net - 3 : net - 2, :]
            b2b[net * H : net * H + H, :] = jnp.transpose(jnp.broadcast_to(0.5 * bias, (128, H)))
        tail = lax.broadcasted_iota(jnp.int32, (K_PAD - OBS, rt), 0)
        ones = jnp.where(tail == ACT, 1.0, 0.0).astype(B16)
        for sub in range(subs):
            xn_all[sub, OBS:K_PAD, :] = ones
            xd_all[sub, OBS:K_PAD, :] = ones
            xq_all[sub, OBS:K_PAD, :] = ones
        acc1[...] = jnp.zeros_like(acc1)
        acc2[...] = jnp.zeros_like(acc2)
        acc_ha[...] = jnp.zeros_like(acc_ha)
        acc_hc[...] = jnp.zeros_like(acc_hc)
        acc_b[...] = jnp.zeros_like(acc_b)
        acc_s[...] = jnp.zeros_like(acc_s)

    def lanes_of(column):
        return jnp.concatenate([column] * lane_tiles, axis=1)

    def lane_sum(value):
        total = value[:, 0:128]
        for tile in range(1, lane_tiles):
            total = total + value[:, tile * 128 : tile * 128 + 128]
        return total

    def biased(source, r, bias_base):
        y = source[r : r + 16, :]
        if bias_base is not None:
            y = y + lanes_of(b2b[bias_base + r : bias_base + r + 16, :])
        return y

    def forward(source, target, rows, bias_base=None):
        for r in range(0, rows, 16):
            target[r : r + 16, :] = gelu_only(biased(source, r, bias_base)).astype(B16)

    def forward_slope(source, target, slope, rows, bias_base=None):
        for r in range(0, rows, 16):
            value, grad = gelu_both(biased(source, r, bias_base))
            target[r : r + 16, :] = value.astype(B16)
            slope[r : r + 16, :] = grad

    def policy(hidden, noise):
        out = dot_nn(wht_a[...].astype(B16), hidden) + lanes_of(hb[0:48, :])
        eps = jnp.concatenate([noise, jnp.zeros((24 - ACT, rt), F32)], axis=0)
        tl = jnp.tanh(out[24:48])
        ls = tl - 1.0
        spread = jnp.exp(ls) * eps
        u = out[0:24] + spread
        act = jnp.tanh(u)
        soft = jnp.maximum(-2.0 * u, 0.0) + jnp.log(1.0 + jnp.exp(-jnp.abs(2.0 * u)))
        terms = -0.5 * eps * eps - ls - HALF_LOG_TAU - 2.0 * (LOG_TWO - u - soft)
        keep = lax.broadcasted_iota(jnp.int32, (24, rt), 0) < ACT
        logp = jnp.sum(jnp.where(keep, terms, 0.0), axis=0, keepdims=True)
        return act, logp, tl, spread

    def head(net, hidden):
        rows = slice(net * 8, net * 8 + 8)
        return dot_nn(wht_c[rows, :].astype(B16), hidden) + lanes_of(hb[48 + net * 8 : 56 + net * 8, :])

    def back_second(source, slope, target, first, last):
        for r in range(first, last, 16):
            d_pre = source[r : r + 16, :] * slope[r : r + 16, :]
            target[r : r + 16, :] = d_pre.astype(B16)
            acc_b[r : r + 16, :] += lane_sum(d_pre)

    def back_first(source, slope, target, first, last):
        for r in range(first, last, 16):
            target[r : r + 16, :] = (source[r : r + 16, :] * slope[r : r + 16, :]).astype(B16)

    def stages(sub):
        cols = slice(sub * rt, sub * rt + rt)
        xn, xd, xq = xn_all.at[sub], xd_all.at[sub], xq_all.at[sub]
        z1, z1q, z2, z2q, zn, zt = (r.at[sub] for r in (z1_all, z1q_all, z2_all, z2q_all, zn_all, zt_all))
        h1n, h2n, h1, h2 = (r.at[sub] for r in (h1n_all, h2n_all, h1_all, h2_all))
        h1q, h2q, h1t, h2t = (r.at[sub] for r in (h1q_all, h2q_all, h1t_all, h2t_all))
        g1, g1q, g2 = (r.at[sub] for r in (g1_all, g1q_all, g2_all))
        dz1, dz2, dzq1, dzq2 = (r.at[sub] for r in (dz1_all, dz2_all, dzq1_all, dzq2_all))

        xn[0:OBS, :] = next_ref[:, cols]
        xd[0:OBS, :] = obs_ref[:, cols]
        xq[0:OBS, :] = obs_ref[:, cols]
        xd[OBS : OBS + ACT, :] = action_ref[:, cols]
        zn[...] = dot_nn(w1t[0:H, :], xn[...])
        z1[...] = dot_nn(w1t[0 : 3 * H, :], xd[...])
        yield
        forward(zn, h1n, H)
        forward_slope(z1, h1, g1, 3 * H)
        yield
        zn[...] = dot_nn(w2t[0:H, :], h1n[...])
        for net in range(3):
            rows = slice(net * H, net * H + H)
            z2[rows, :] = dot_nn(w2t[rows, :], h1[rows, :])
        forward(zn, h2n, H, 0)
        forward_slope(z2, h2, g2, 3 * H, 0)
        yield
        index = t_index * (n_steps * subs * rt) + (step * subs + sub) * rt
        index = index + lax.broadcasted_iota(jnp.int32, (1, rt), 1)
        valid = (index < count_ref[0]).astype(F32)
        alpha = jnp.exp(jnp.full((1, rt), state_ref[0], F32))
        omega = state_ref[3] * state_ref[3]
        act_next, logp_next, _, _ = policy(h2n[...], next_noise_ref[:, cols])
        act_new, logp_new, tl_new, spread_new = policy(h2[0:H, :], noise_ref[:, cols])
        xn[OBS : OBS + ACT, :] = act_next[0:ACT].astype(B16)
        xq[OBS : OBS + ACT, :] = act_new[0:ACT].astype(B16)
        zt[...] = dot_nn(w1t[3 * H : 5 * H, :], xn[...])
        z1q[...] = dot_nn(w1t[H : 3 * H, :], xq[...])
        yield
        forward(zt, h1t, 2 * H)
        forward_slope(z1q, h1q, g1q, 2 * H)
        yield
        for net in range(2):
            rows = slice(net * H, net * H + H)
            zt[rows, :] = dot_nn(w2t[(3 + net) * H : (4 + net) * H, :], h1t[rows, :])
            z2q[rows, :] = dot_nn(w2t[(1 + net) * H : (2 + net) * H, :], h1q[rows, :])
        forward(zt, h2t, 2 * H, 3 * H)
        for r in range(0, 2 * H, 16):
            value, grad = gelu_both(biased(z2q, r, H))
            h2q[r : r + 16, :] = value.astype(B16)
            dzq2[r : r + 16, :] = (lanes_of(wqb[r : r + 16, :]) * grad).astype(B16)
        yield
        out_t = [head(2 + net, h2t[net * H : net * H + H, :])[0:1] for net in range(2)]
        out_d = [head(net, h2[(1 + net) * H : (2 + net) * H, :]) for net in range(2)]
        out_q = [head(net, h2q[net * H : net * H + H, :])[0:1] for net in range(2)]
        for net in range(2):
            rows = slice(net * H, net * H + H)
            z1q[rows, :] = dot_nn(w2[(1 + net) * H : (2 + net) * H, :], dzq2[rows, :])
        alive = 1.0 - terminal_ref[:, cols].astype(F32)
        target = reward_ref[:, cols] + GAMMA * alive * (jnp.minimum(out_t[0], out_t[1]) - alpha * logp_next)
        loss_row = valid * (alpha * logp_new - 0.5 * (out_q[0] + out_q[1]))
        sigma_row = jnp.zeros((1, rt), F32)
        next_row = valid * (logp_next - ACT)
        d_heads = []
        for net in range(2):
            log_sigma = jnp.tanh(out_d[net][1:2])
            sigma = jnp.exp(log_sigma)
            error = target - out_d[net][0:1]
            inverse = 1.0 / (sigma * sigma)
            scaled = error * inverse
            square = error * scaled
            loss_row = loss_row + valid * (omega * (0.5 * square + log_sigma))
            sigma_row = sigma_row + valid * sigma
            d_q = -(omega * valid) * scaled
            d_s = (omega * valid) * (1.0 - square) * (1.0 - log_sigma * log_sigma)
            d_heads.append(jnp.concatenate([d_q, d_s, jnp.zeros((6, rt), F32)], axis=0).astype(B16))
        acc_s[64:65, :] += lane_sum(loss_row)
        acc_s[72:73, :] += lane_sum(sigma_row)
        acc_s[80:81, :] += lane_sum(next_row)
        yield
        for net in range(2):
            rows = slice((1 + net) * H, (2 + net) * H)
            acc_s[48 + net * 8 : 56 + net * 8, :] += lane_sum(d_heads[net].astype(F32))
            acc_hc[net * 8 : net * 8 + 8, :] += dot_nt(d_heads[net], h2[rows, :])
            z2[rows, :] = dot_nn(wh_c[:, net * 8 : net * 8 + 8], d_heads[net])
        back_first(z1q, g1q, dzq1, 0, 2 * H)
        d_act = dot_nn(w1a[0:32, :], dzq1[0:H, :]) + dot_nn(w1a[32:64, :], dzq1[H : 2 * H, :])
        back_second(z2, g2, dz2, H, 3 * H)
        yield
        d_act = d_act[0:24] * (-0.5 * valid)
        d_logp = alpha * valid
        d_u = d_act * (1.0 - act_new * act_new) + (2.0 * d_logp) * act_new
        d_ls = (d_u * spread_new - d_logp) * (1.0 - tl_new * tl_new)
        d_out = jnp.concatenate([d_u, d_ls], axis=0).astype(B16)
        acc_s[0:48, :] += lane_sum(d_out.astype(F32))
        acc_ha[...] += dot_nt(d_out, h2[0:H, :])
        z2[0:H, :] = dot_nn(wh_a[...], d_out)
        for net in range(1, 3):
            rows = slice(net * H, net * H + H)
            z1[rows, :] = dot_nn(w2[rows, :], dz2[rows, :])
        back_second(z2, g2, dz2, 0, H)
        z1[0:H, :] = dot_nn(w2[0:H, :], dz2[0:H, :])
        back_first(z1, g1, dz1, H, 3 * H)
        yield
        back_first(z1, g1, dz1, 0, H)
        for net in (1, 2, 0):
            rows = slice(net * H, net * H + H)
            acc2[rows, :] += dot_nt(h1[rows, :], dz2[rows, :])
        acc1[...] += dot_nt(xd[0:K_USE, :], dz1[...])

    running = [stages(sub) for sub in range(subs)]
    alive_count = subs
    turn = 0
    done = [False] * subs
    while alive_count:
        for sub in range(subs):
            if not done[sub] and turn >= sub * offset:
                if next(running[sub], "end") == "end":
                    done[sub] = True
                    alive_count -= 1
        turn += 1

    @pl.when(step == n_steps - 1)
    def _():
        mine, others = own_chunk(orders), own_chunk(orders[::-1])
        flat[:, FLAT_SMALL:FLAT_ROWS, :] = jnp.zeros((2, FLAT_ROWS - FLAT_SMALL, 128), F32)
        flat[:, FLAT_AW1 - 8 : FLAT_AW1, :] = jnp.zeros((2, 8, 128), F32)
        flat[:, FLAT_AW2 - 8 : FLAT_AW2, :] = jnp.zeros((2, 8, 128), F32)
        sums = jnp.sum(jnp.transpose(acc_s[...]), axis=0, keepdims=True)
        lane = lax.broadcasted_iota(jnp.int32, (1, 128), 1)
        keep = (lane < ACT) | ((lane >= 24) & (lane < 24 + ACT)) | ((lane >= 48) & (lane < 50))
        keep = keep | ((lane >= 56) & (lane < 58)) | (lane == LANE_LOSS) | (lane == LANE_SIGMA) | (lane == LANE_NEXT)
        sums = jnp.where(keep, sums, 0.0)
        sums = jnp.where(lane == LANE_COUNT, 0.5 * count_ref[0].astype(F32), sums)
        for side in range(2):
            lanes = slice(side * HALF, side * HALF + HALF)
            for net in range(2):
                columns = slice((1 + net) * H + side * HALF, (1 + net) * H + side * HALF + HALF)
                flat[side, pl.ds(FLAT_CW1 + net, C_IN, stride=2), :] = acc1[0:C_IN, columns]
            flat[side, FLAT_AW1 : FLAT_AW1 + OBS, :] = acc1[0:OBS, lanes]
            flat[side, FLAT_AW1 + OBS : FLAT_AW1 + A_IN, :] = acc1[BIAS_ROW : BIAS_ROW + 1, lanes]
            for net in range(3):
                rows = slice(net * H + side * HALF, net * H + side * HALF + HALF)
                for part in range(2):
                    base = FLAT_AW2 + (net * 2 + part) * HALF
                    flat[side, base : base + HALF, :] = acc2[rows, part * 128 : part * 128 + 128]
            for part in range(2):
                cols = slice(part * 128, part * 128 + 128)
                base = FLAT_AHEAD + part * 40
                flat[side, base : base + ACT, :] = acc_ha[0:ACT, cols]
                flat[side, base + ACT : base + 2 * ACT, :] = acc_ha[24 : 24 + ACT, cols]
                for net in range(2):
                    base = FLAT_CHEAD + part * 4 + net * 2
                    flat[side, base : base + 2, :] = acc_hc[net * 8 : net * 8 + 2, cols]
            for net in range(3):
                for part in range(2):
                    rows = slice(net * H + part * 128, net * H + part * 128 + 128)
                    row = FLAT_B2 + part * 4 + net
                    flat[side, row : row + 1, :] = jnp.sum(jnp.transpose(acc_b[rows, :]), axis=0, keepdims=True)
            flat[side, FLAT_SUMS : FLAT_SUMS + 1, :] = sums
        size = FLAT_ROWS // len(order)
        per = len(order) // n_own
        for place, rel in enumerate(order):
            start = pl.multiple_of(jnp.bitwise_xor(mine, rel) * size, size)
            own_outs[place // per][(place % per) * size : (place % per) * size + size, :] = flat[0, pl.ds(start, size), :]
            start = pl.multiple_of(jnp.bitwise_xor(others, rel) * size, size)
            par_out[place * size : place * size + size, :] = flat[1, pl.ds(start, size), :]


SUB_ROWS = 256
SUBS = 2
SUB_OFFSET = 2


def run_step(groups, arrays, pack_own, pack_par, small, count, state):
    obs, next_obs, action, noise, next_noise, reward, terminal = arrays
    rows = obs.shape[1] // groups["tensor"]
    rt = min(SUB_ROWS, rows)
    subs = min(SUBS, rows // rt)
    steps = rows // (rt * subs)
    order, n_own = groups["order"], groups["first"]

    def tile(height):
        return pl.BlockSpec((height, rt * subs), lambda i: (0, lax.axis_index("tensor") * steps + i))

    def each(height, dtype):
        return VMEM((subs, height, rt), dtype)

    whole = pl.BlockSpec(memory_space=VMEM)
    smem = pl.BlockSpec(memory_space=pltpu.SMEM)
    scratch = [
        VMEM((5 * H, K_PAD), B16), VMEM((5 * H, H), B16), VMEM((5 * H, H), B16), VMEM((64, H), B16),
        VMEM((48, H), F32), VMEM((H, 48), B16), VMEM((32, H), F32), VMEM((H, 32), B16),
        VMEM((80, 128), F32), VMEM((5 * H, 128), F32), VMEM((2 * H, 128), F32),
        each(K_PAD, B16), each(K_PAD, B16), each(K_PAD, B16),
        each(3 * H, F32), each(2 * H, F32), each(3 * H, F32), each(2 * H, F32), each(H, F32), each(2 * H, F32),
        each(H, B16), each(H, B16), each(3 * H, B16), each(3 * H, B16),
        each(2 * H, B16), each(2 * H, B16), each(2 * H, B16), each(2 * H, B16),
        each(3 * H, F32), each(2 * H, F32), each(3 * H, F32),
        each(3 * H, B16), each(3 * H, B16), each(2 * H, B16), each(2 * H, B16),
        VMEM((K_USE, 3 * H), F32), VMEM((3 * H, H), F32), VMEM((48, H), F32), VMEM((16, H), F32),
        VMEM((3 * H, 128), F32), VMEM((128, 128), F32), VMEM((2, FLAT_ROWS, 128), F32),
    ]
    outs = [jax.ShapeDtypeStruct((FLAT_ROWS // n_own, 128), F32)] * n_own + [jax.ShapeDtypeStruct((FLAT_ROWS, 128), F32)]
    return pl.pallas_call(
        functools.partial(step_kernel, rt, subs, SUB_OFFSET, order, groups["orders"], n_own),
        grid=(steps,),
        in_specs=[smem, smem, tile(OBS), tile(OBS), tile(ACT), tile(ACT), tile(ACT), tile(1), tile(1)] + [whole] * 7,
        out_specs=[whole] * (n_own + 1),
        out_shape=outs,
        scratch_shapes=scratch,
        compiler_params=pltpu.CompilerParams(vmem_limit_bytes=STEP_VMEM),
        name="step",
    )(
        count, state, *in_hbm(obs, next_obs, action, noise, next_noise, reward, terminal),
        pack_own, pack_par, *in_hbm(*small),
    )


def last_sum_kernel(size, n_in, orders, *refs):
    out = refs[n_in]
    first = own_chunk(orders) * size
    part = jnp.zeros((8, 128), F32)
    lane = lax.broadcasted_iota(jnp.int32, (8, 128), 1)
    for r in range(0, size, 8):
        total = refs[0][r : r + 8, :]
        for ref in refs[1:n_in]:
            total = total + ref[r : r + 8, :]
        out[r : r + 8, :] = total
        row = first + r + lax.broadcasted_iota(jnp.int32, (8, 128), 0)
        weight = jnp.where(row < FLAT_SMALL, 1.0, 0.5)
        weight = jnp.where((row >= FLAT_SUMS) & (lane >= LANE_LOSS), 0.0, weight)
        part = part + total * total * weight
    out[size : size + 8, :] = part


def last_sum(values, orders):
    size = values[0].shape[0]
    return pl.pallas_call(
        functools.partial(last_sum_kernel, size, len(values), orders),
        out_shape=jax.ShapeDtypeStruct((size + 8, 128), F32),
        compiler_params=pltpu.CompilerParams(vmem_limit_bytes=SMALL_VMEM),
        name="lastsum",
    )(*values)


def one_minus_power(gap, exponent):
    total = jnp.float32(0.0)
    for bit in range(30, -1, -1):
        total = total * (2.0 - total)
        total = jnp.where((exponent >> bit) & 1 == 1, total + gap * (1.0 - total), total)
    return total


def update_kernel(order, orders, n_parts, sizes, *refs):
    parts = refs[:n_parts]
    (
        square_own, square_other, step_ref, state_ref,
        a_w1, a_w1_m, a_w2, a_w2_m, a_head, a_head_m,
        c_w1, c_w1_m, c_w2, c_w2_m, c_head, c_head_m, bias2, bias2_m,
        t_w1, t_w2, t_head, t_bias2,
        o_a_w1, o_a_w1_f, o_a_w1_s, o_a_w2, o_a_w2_f, o_a_w2_s, o_a_head, o_a_head_f, o_a_head_s,
        o_c_w1, o_c_w1_f, o_c_w1_s, o_c_w2, o_c_w2_f, o_c_w2_s, o_c_head, o_c_head_f, o_c_head_s,
        o_bias2, o_bias2_f, o_bias2_s, o_scalars, o_norm,
        flat, rows_new, rows_target,
    ) = refs[n_parts:]
    size, stride = sizes
    mine = own_chunk(orders)
    per = len(order) // n_parts
    square = square_own[...] + square_other[...]
    for place, rel in enumerate(order):
        start = pl.multiple_of(jnp.bitwise_xor(mine, rel) * size, size)
        base = (place % per) * stride
        flat[pl.ds(start, size), :] = parts[place // per][base : base + size, :]
    sums = flat[FLAT_SUMS : FLAT_SUMS + 1, :]
    lane = lax.broadcasted_iota(jnp.int32, (1, 128), 1)

    def pick(index):
        return jnp.sum(jnp.where(lane == index, sums, 0.0), axis=1, keepdims=True)

    loss_sum, sigma_sum, next_sum, count = (pick(i) for i in (LANE_LOSS, LANE_SIGMA, LANE_NEXT, LANE_COUNT))
    inverse = 1.0 / count
    total = jnp.sum(jnp.sum(square, axis=0, keepdims=True), axis=1, keepdims=True)
    norm = jnp.sqrt(total) * inverse
    clip = jnp.minimum(1.0, CLIP / (norm + 1e-06))
    scale = clip * inverse
    t = step_ref[0]
    first_fix = one_minus_power(jnp.float32(0.1), t)
    second_fix = one_minus_power(jnp.float32(0.001), t)
    unfix_one = 1.0 / jnp.full((1, 1), first_fix, F32)
    unfix_two = 1.0 / jnp.full((1, 1), second_fix, F32)

    def adam(weight, first, second, grad, decay=DECAY):
        first = BETA_ONE * first + (1.0 - BETA_ONE) * grad
        second = BETA_TWO * second + (1.0 - BETA_TWO) * (grad * grad)
        step = first * unfix_one / (jnp.sqrt(second * unfix_two) + ADAM_EPS)
        if decay:
            step = step + decay * weight
        return weight - RATE * step, first, second

    def polyak(target, new):
        return (1.0 - RHO) * target + RHO * new

    moments = a_w1_m.reshape(2 * A_IN, 128)
    new, first, second = adam(
        a_w1[...], moments[pl.ds(0, A_IN, stride=2), :], moments[pl.ds(1, A_IN, stride=2), :],
        flat[FLAT_AW1 : FLAT_AW1 + A_IN, :] * scale,
    )
    o_a_w1[...] = new
    o_a_w1_f[...] = first
    o_a_w1_s[...] = second
    for net in range(3):
        for part in range(2):
            lanes = slice(part * 128, part * 128 + 128)
            base = FLAT_AW2 + (net * 2 + part) * HALF
            grad = flat[base : base + HALF, :] * scale
            if net == 0:
                new, first, second = adam(a_w2[:, lanes], a_w2_m[0, :, lanes], a_w2_m[1, :, lanes], grad)
                o_a_w2[:, lanes] = new
                o_a_w2_f[:, lanes] = first
                o_a_w2_s[:, lanes] = second
            else:
                c = net - 1
                new, first, second = adam(c_w2[c, :, lanes], c_w2_m[0, c, :, lanes], c_w2_m[1, c, :, lanes], grad)
                o_c_w2[c, :, lanes] = new
                o_c_w2[2 + c, :, lanes] = polyak(t_w2[c, :, lanes], new)
                o_c_w2_f[c, :, lanes] = first
                o_c_w2_s[c, :, lanes] = second
    both = 2 * C_IN
    new, first, second = adam(
        c_w1.reshape(both, 128)[...], c_w1_m.at[0].reshape(both, 128)[...], c_w1_m.at[1].reshape(both, 128)[...],
        flat[FLAT_CW1 : FLAT_CW1 + both, :] * scale,
    )
    o_c_w1_f.reshape(both, 128)[...] = first
    o_c_w1_s.reshape(both, 128)[...] = second
    rows_new[...] = new
    rows_target[...] = polyak(t_w1.reshape(both, 128)[...], new)
    four = o_c_w1.reshape(2 * both, 128)
    for c in range(2):
        four[pl.ds(c, C_IN, stride=4), :] = rows_new[pl.ds(c, C_IN, stride=2), :]
        four[pl.ds(2 + c, C_IN, stride=4), :] = rows_target[pl.ds(c, C_IN, stride=2), :]
    columns = jnp.transpose(jnp.broadcast_to(sums, (128, 128)))
    bias_a = jnp.concatenate([columns[0:ACT, 0:1], columns[24 : 24 + ACT, 0:1]], axis=0)
    grad = jnp.concatenate(
        [flat[FLAT_AHEAD : FLAT_AHEAD + 2 * ACT, :], flat[FLAT_AHEAD + 40 : FLAT_AHEAD + 40 + 2 * ACT, :], bias_a], axis=1
    )
    new, first, second = adam(a_head[...], a_head_m[:, 0, :], a_head_m[:, 1, :], grad * scale)
    o_a_head[...] = new
    o_a_head_f[...] = first
    o_a_head_s[...] = second
    for c in range(2):
        rows = slice(FLAT_CHEAD + c * 2, FLAT_CHEAD + c * 2 + 2)
        rows_b = slice(FLAT_CHEAD + 4 + c * 2, FLAT_CHEAD + 6 + c * 2)
        bias_c = columns[LANE_C + 8 * c : LANE_C + 8 * c + 2, 0:1]
        grad = jnp.concatenate([flat[rows, :], flat[rows_b, :], bias_c], axis=1) * scale
        new, first, second = adam(c_head[c], c_head_m[0, c], c_head_m[1, c], grad)
        o_c_head[c] = new
        o_c_head[2 + c] = polyak(t_head[c], new)
        o_c_head_f[c] = first
        o_c_head_s[c] = second
    grad = jnp.concatenate([flat[FLAT_B2 : FLAT_B2 + 3, :], flat[FLAT_B2 + 4 : FLAT_B2 + 7, :]], axis=1) * scale
    new, first, second = adam(bias2[...], bias2_m[:, 0, :], bias2_m[:, 1, :], grad)
    o_bias2[0:3, :] = new
    o_bias2[3:5, :] = polyak(t_bias2[...], new[1:3])
    o_bias2_f[...] = first
    o_bias2_s[...] = second
    log_alpha = jnp.full((1, 1), state_ref[0], F32)
    g_alpha = -next_sum
    new, first, second = adam(
        log_alpha, jnp.full((1, 1), state_ref[1], F32), jnp.full((1, 1), state_ref[2], F32), g_alpha * inverse, 0.0
    )
    stat = (1.0 - TAU_STAT) * state_ref[3] + TAU_STAT * sigma_sum / (2.0 * count)
    loss = (loss_sum + log_alpha * g_alpha) * inverse
    for place, value in enumerate((new, first, second, stat, loss)):
        o_scalars[place] = value[0, 0]
    o_norm[0] = norm[0, 0]


def shards(
    groups, obs, action, next_obs, reward, terminal, noise, next_noise, counts, step_count,
    a_w1, a_w2, a_head, c_w1, c_w2, c_head, bias2, tc_w1, tc_w2, tc_head, tc_bias2,
    a_w1_mom, a_w2_mom, a_head_mom, c_w1_mom, c_w2_mom, c_head_mom, bias2_mom, state,
):
    n_dp = groups["dp"]
    swap = [(0, 1), (1, 0)]

    def partner(value):
        return lax.ppermute(value, "tensor", swap)

    def across(value, phase, k):
        masks = [sum(((k >> place) & 1) << bit for place, bit in enumerate(bits)) for bits in phase]
        pairs = [(2 * d + t, 2 * (d ^ masks[t]) + t) for d in range(n_dp) for t in range(2)]
        return lax.ppermute(value, ("dp", "tensor"), pairs)

    tr = jnp.transpose
    c_w1v, tc_w1v = tr(c_w1, (1, 0, 2)), tr(tc_w1, (1, 0, 2))
    a_headv, c_headv, tc_headv = tr(a_head), tr(c_head, (0, 2, 1)), tr(tc_head, (0, 2, 1))
    pack = pack_weights(a_w1, c_w1v, tc_w1v, a_w2, c_w2, tc_w2)
    pack_par = partner(pack)
    arrays = (
        tr(obs), tr(next_obs), tr(action), tr(noise), tr(next_noise), reward.reshape(1, -1), terminal.reshape(1, -1),
    )
    small = (a_headv, c_headv, tc_headv, bias2, tc_bias2)
    outs = run_step(groups, arrays, pack, pack_par, small, counts, state)
    own, par = outs[:-1], outs[-1]
    received = partner(par)
    size = FLAT_ROWS // len(own)
    values = [item + received[i * size : i * size + size] for i, item in enumerate(own)]

    *scatters, last = groups["phases"]
    following = [1 << len(phase[0]) for phase in scatters[1:]] + [1]
    for phase, ways_next in zip(scatters, following):
        got = [values[0]] + [across(values[k], phase, k) for k in range(1, 1 << len(phase[0]))]
        size = got[0].shape[0] // ways_next
        values = [sum(item[j * size : j * size + size] for item in got) for j in range(ways_next)]
    got = [values[0]] + [across(values[0], last, k) for k in range(1, 1 << len(last[0]))]
    block = last_sum(got, groups["orders"])
    for number, phase in reversed(list(enumerate(scatters))):
        got = [block] + [across(block, phase, k) for k in range(1, 1 << len(phase[0]))]
        if number:
            block = jnp.concatenate(got)
    parts = got
    own_square = sum(
        part[r + size : r + size + 8] for part in parts for r in range(0, part.shape[0], size + 8)
    )
    other_square = partner(own_square)

    sds = jax.ShapeDtypeStruct
    shapes = [
        (A_IN, HALF)] * 3 + [(HALF, H)] * 3 + [(2 * ACT, H + 1)] * 3 + [
        (C_IN, 4, HALF), (C_IN, 2, HALF), (C_IN, 2, HALF),
        (4, HALF, H), (2, HALF, H), (2, HALF, H),
        (4, 2, H + 1), (2, 2, H + 1), (2, 2, H + 1),
        (5, H), (3, H), (3, H), (5,), (1,),
    ]
    whole = pl.BlockSpec(memory_space=VMEM)
    smem = pl.BlockSpec(memory_space=pltpu.SMEM)
    res = pl.pallas_call(
        functools.partial(update_kernel, groups["order"], groups["orders"], len(parts), (size, size + 8)),
        in_specs=[whole] * (len(parts) + 2) + [smem, smem] + [whole] * 18,
        out_specs=[whole] * 21 + [smem, smem],
        out_shape=[sds(s, F32) for s in shapes],
        scratch_shapes=[VMEM((FLAT_ROWS, 128), F32), VMEM((2 * C_IN, 128), F32), VMEM((2 * C_IN, 128), F32)],
        compiler_params=pltpu.CompilerParams(vmem_limit_bytes=UPDATE_VMEM),
        name="update",
    )(
        *parts, own_square, other_square, step_count, state,
        a_w1, tr(a_w1_mom, (1, 0, 2)), a_w2, a_w2_mom, a_headv, tr(a_head_mom, (2, 0, 1)),
        c_w1v, tr(c_w1_mom, (0, 2, 1, 3)), c_w2, c_w2_mom, c_headv, tr(c_head_mom, (0, 1, 3, 2)),
        bias2, tr(bias2_mom, (1, 0, 2)), tc_w1v, tc_w2, tc_headv, tc_bias2,
    )
    res = list(res)
    for place in (6, 7, 8):
        res[place] = tr(res[place])
    for place in (9, 10, 11):
        res[place] = tr(res[place], (1, 0, 2))
    for place in (15, 16, 17):
        res[place] = tr(res[place], (0, 2, 1))
    return tuple(res)


def plan(mesh):
    n_dp = mesh.shape["dp"]
    bits = n_dp.bit_length() - 1
    assert n_dp == 1 << bits and mesh.shape["tensor"] == 2
    groups = [tuple(range(low, min(low + 2, bits))) for low in range(0, bits, 2)]
    assert len(groups) > 1
    pairs = [group for group in groups if len(group) == 2]
    turned = pairs[1:] + pairs[:1] + groups[len(pairs) :]
    phases = list(zip(groups, turned))
    order = [0]
    low = 0
    for group in groups[:-1]:
        order = [rel | (k << low) for rel in order for k in range(1 << len(group))]
        low += len(group)
    return {
        "dp": n_dp,
        "tensor": mesh.shape["tensor"],
        "phases": phases,
        "order": tuple(order),
        "orders": tuple(tuple(bit for group in core[:-1] for bit in group) for core in (groups, turned)),
        "first": 1 << len(groups[0]),
    }


def solution(mesh):
    in_specs = (
        P("dp", None), P("dp", None), P("dp", None), P("dp"), P("dp"), P("dp", None), P("dp", None), P("dp"), P(),
        P(None, "tensor"), P("tensor", None), P(), P(None, None, "tensor"), P(None, "tensor", None), P(), P(),
        P(None, None, "tensor"), P(None, "tensor", None), P(), P(),
        P(None, None, "tensor"), P(None, "tensor", None), P(), P(None, None, None, "tensor"),
        P(None, None, "tensor", None), P(), P(), P(),
    )
    out_specs = (
        P(None, "tensor"), P(None, "tensor"), P(None, "tensor"),
        P("tensor", None), P("tensor", None), P("tensor", None),
        P(), P(), P(),
        P(None, None, "tensor"), P(None, None, "tensor"), P(None, None, "tensor"),
        P(None, "tensor", None), P(None, "tensor", None), P(None, "tensor", None),
        P(), P(), P(), P(), P(), P(), P(), P(),
    )
    return jax.shard_map(
        functools.partial(shards, plan(mesh)), mesh=mesh, in_specs=in_specs, out_specs=out_specs, check_vma=False
    )
```

```python
import functools
import math

import jax
import jax.numpy as jnp
from jax import lax
from jax.experimental import pallas as pl
from jax.experimental.pallas import tpu as pltpu
from jax.sharding import PartitionSpec as P

OBS = 376
ACT = 17
H = 256
GAMMA = 0.99
RHO = 0.005
TAU_STAT = 0.1
CLIP = 0.005
RATE = 0.05
BETA_ONE = 0.9
BETA_TWO = 0.999
ADAM_EPS = 1e-08
DECAY = 0.01
HALF_LOG_TAU = 0.5 * math.log(2.0 * math.pi)
LOG_TWO = math.log(2.0)
GELU_A = math.sqrt(2.0 / math.pi)
GELU_B = GELU_A * 0.044715
F32 = jnp.float32
B16 = jnp.bfloat16

A_IN = OBS + 1
C_IN = OBS + ACT + 1
BIAS_ROW = OBS + ACT
K_PAD = 512
K_USE = 400
HALF = H // 2
VMEM = pltpu.VMEM
STEP_VMEM = 50 * 1024 * 1024
UPDATE_VMEM = 24 * 1024 * 1024
SMALL_VMEM = 8 * 1024 * 1024

PACK_W2 = 5 * 4 * HALF
PACK_ACT = PACK_W2 + 5 * 2 * HALF
PACK_ROWS = PACK_ACT + 2 * 32

FLAT_CW1 = 0
FLAT_AW1 = 792
FLAT_AW2 = FLAT_AW1 + 384
FLAT_CW2 = FLAT_AW2 + H
FLAT_SMALL = FLAT_CW2 + 2 * H
FLAT_AHEAD = FLAT_SMALL
FLAT_CHEAD = FLAT_AHEAD + 80
FLAT_B2 = FLAT_CHEAD + 8
FLAT_SUMS = FLAT_B2 + 8
FLAT_ROWS = FLAT_SUMS + 8
LANE_C = 48
LANE_LOSS = 64
LANE_SIGMA = 72
LANE_NEXT = 80
LANE_COUNT = 88


def dot_nn(a, b):
    return lax.dot_general(a, b, (((1,), (0,)), ((), ())), preferred_element_type=F32)


def dot_nt(a, b):
    return lax.dot_general(a, b, (((1,), (1,)), ((), ())), preferred_element_type=F32)


def gelu_only(y):
    t = jnp.tanh(y * (2.0 * GELU_A + (8.0 * GELU_B) * (y * y)))
    return y * (1.0 + t)


def gelu_both(y):
    w = y * y
    t = jnp.tanh(y * (2.0 * GELU_A + (8.0 * GELU_B) * w))
    e = 1.0 + t
    value = y * e
    return value, e + (value * (1.0 - t)) * (2.0 * GELU_A + (24.0 * GELU_B) * w)


def own_chunk(orders):
    d_index = lax.axis_index("dp")
    found = []
    for order in orders:
        number = jnp.int32(0)
        for place, bit in enumerate(order):
            number = number | (((d_index >> bit) & 1) << place)
        found.append(number)
    return jnp.where(lax.axis_index("tensor") == 0, found[0], found[1])


def pack_kernel(a_w1, c_w1, t_w1, a_w2, c_w2, t_w2, out, wide):
    for net in range(5):
        wide[...] = jnp.zeros_like(wide)
        if net == 0:
            wide[0:OBS, :] = a_w1[0:OBS, :]
            wide[BIAS_ROW : BIAS_ROW + 1, :] = a_w1[OBS:A_IN, :]
        else:
            source = c_w1 if net < 3 else t_w1
            wide[0:C_IN, :] = source.reshape(2 * C_IN, 128)[pl.ds((net - 1) % 2, C_IN, stride=2), :]
        for tile in range(4):
            base = (net * 4 + tile) * HALF
            out[base : base + HALF, :] = jnp.transpose(0.5 * wide[tile * 128 : tile * 128 + 128, :]).astype(B16)
        if net in (1, 2):
            base = PACK_ACT + (net - 1) * 32
            rows = lax.broadcasted_iota(jnp.int32, (32, 128), 0)
            out[base : base + 32, :] = jnp.where(rows < ACT, wide[OBS : OBS + 32, :], 0.0).astype(B16)
        for part in range(2):
            base = PACK_W2 + (net * 2 + part) * HALF
            lanes = slice(part * 128, part * 128 + 128)
            if net == 0:
                block = a_w2[:, lanes]
            else:
                block = (c_w2 if net < 3 else t_w2)[(net - 1) % 2, :, lanes]
            out[base : base + HALF, :] = (0.5 * block).astype(B16)


def in_hbm(*values):
    return [pltpu.with_memory_space_constraint(value, pltpu.HBM) for value in values]


def pack_weights(a_w1, c_w1, t_w1, a_w2, c_w2, t_w2):
    return pl.pallas_call(
        pack_kernel,
        out_shape=jax.ShapeDtypeStruct((PACK_ROWS, 128), B16),
        scratch_shapes=[VMEM((K_PAD, 128), F32)],
        compiler_params=pltpu.CompilerParams(vmem_limit_bytes=SMALL_VMEM),
        name="pack",
    )(*in_hbm(a_w1, c_w1, t_w1, a_w2, c_w2, t_w2))


def one_minus_power(gap, exponent):
    total = jnp.float32(0.0)
    for bit in range(30, -1, -1):
        total = total * (2.0 - total)
        total = jnp.where((exponent >> bit) & 1 == 1, total + gap * (1.0 - total), total)
    return total


def step_kernel(
    rows_tile,
    subs,
    offset,
    order,
    orders,
    n_own,
    count_ref,
    state_ref,
    when_ref,
    obs_ref,
    next_ref,
    action_ref,
    noise_ref,
    next_noise_ref,
    reward_ref,
    terminal_ref,
    pack_own,
    pack_par,
    a_head_ref,
    c_head_ref,
    t_head_ref,
    bias2_ref,
    t_bias2_ref,
    *rest,
):
    own_outs = rest[:n_own]
    par_out, fix_out = rest[n_own : n_own + 2]
    (
        w1t, w2, w2t, w1a, wht_a, wh_a, wht_c, wh_c, hb, b2b, wqb,
        xn_all, xd_all, xq_all,
        z1_all, z1q_all, z2_all, z2q_all, zn_all, zt_all,
        h1n_all, h2n_all, h1_all, h2_all, h1q_all, h2q_all, h1t_all, h2t_all,
        g1_all, g1q_all, g2_all, dz1_all, dz2_all, dzq1_all, dzq2_all,
        acc1, acc2, acc_ha, acc_hc, acc_b, acc_s, flat,
    ) = rest[n_own + 2 :]
    step = pl.program_id(0)
    n_steps = pl.num_programs(0)
    t_index = lax.axis_index("tensor")
    rt = rows_tile
    lane_tiles = rt // 128

    @pl.when(step == 0)
    def _():
        for row, gap in enumerate((0.1, 0.001)):
            fix = one_minus_power(jnp.float32(gap), when_ref[0])
            fix_out[row : row + 1, :] = 1.0 / jnp.full((1, 128), fix, F32)
        for net in range(5):
            for side, pack in enumerate((pack_own, pack_par)):
                rows = slice(net * H + side * HALF, net * H + side * HALF + HALF)
                for tile in range(4):
                    base = (net * 4 + tile) * HALF
                    w1t[rows, tile * 128 : tile * 128 + 128] = pack[base : base + HALF, :]
                for part in range(2):
                    base = PACK_W2 + (net * 2 + part) * HALF
                    w2[rows, part * 128 : part * 128 + 128] = pack[base : base + HALF, :]
        for side, pack in enumerate((pack_own, pack_par)):
            w1a[:, side * HALF : side * HALF + HALF] = pack[PACK_ACT:PACK_ROWS, :]
        for net in range(5):
            w2t[net * H : net * H + H, :] = jnp.transpose(w2[net * H : net * H + H, :])
        wht_a[...] = jnp.zeros_like(wht_a)
        hb[...] = jnp.zeros_like(hb)
        for part in range(2):
            rows = a_head_ref[part * ACT : part * ACT + ACT, :].astype(B16)
            wht_a[part * 24 : part * 24 + ACT, :] = rows[:, 0:H].astype(F32)
            hb[part * 24 : part * 24 + ACT, :] = jnp.broadcast_to(rows[:, H : H + 1].astype(F32), (ACT, 128))
        wh_a[...] = jnp.transpose(0.5 * wht_a[...]).astype(B16)
        wht_c[...] = jnp.zeros_like(wht_c)
        for net in range(4):
            head = (c_head_ref if net < 2 else t_head_ref)[net % 2].astype(B16).astype(F32)
            wht_c[net * 8 : net * 8 + 2, :] = head[:, 0:H]
            hb[48 + net * 8 : 48 + net * 8 + 2, :] = jnp.broadcast_to(head[:, H : H + 1], (2, 128))
        wh_c[...] = jnp.transpose(0.5 * wht_c[...]).astype(B16)
        for net in range(2):
            row = 0.5 * wht_c[net * 8 : net * 8 + 1, :]
            wqb[net * H : net * H + H, :] = jnp.transpose(jnp.broadcast_to(row, (128, H)))
        for net in range(5):
            bias = bias2_ref[net : net + 1, :] if net < 3 else t_bias2_ref[net - 3 : net - 2, :]
            b2b[net * H : net * H + H, :] = jnp.transpose(jnp.broadcast_to(0.5 * bias, (128, H)))
        tail = lax.broadcasted_iota(jnp.int32, (K_PAD - OBS, rt), 0)
        ones = jnp.where(tail == ACT, 1.0, 0.0).astype(B16)
        for sub in range(subs):
            xn_all[sub, OBS:K_PAD, :] = ones
            xd_all[sub, OBS:K_PAD, :] = ones
            xq_all[sub, OBS:K_PAD, :] = ones
        acc1[...] = jnp.zeros_like(acc1)
        acc2[...] = jnp.zeros_like(acc2)
        acc_ha[...] = jnp.zeros_like(acc_ha)
        acc_hc[...] = jnp.zeros_like(acc_hc)
        acc_b[...] = jnp.zeros_like(acc_b)
        acc_s[...] = jnp.zeros_like(acc_s)

    def lanes_of(column):
        return jnp.concatenate([column] * lane_tiles, axis=1)

    def lane_sum(value):
        total = value[:, 0:128]
        for tile in range(1, lane_tiles):
            total = total + value[:, tile * 128 : tile * 128 + 128]
        return total

    def biased(source, r, bias_base):
        y = source[r : r + 16, :]
        if bias_base is not None:
            y = y + lanes_of(b2b[bias_base + r : bias_base + r + 16, :])
        return y

    def forward(source, target, rows, bias_base=None):
        for r in range(0, rows, 16):
            target[r : r + 16, :] = gelu_only(biased(source, r, bias_base)).astype(B16)

    def forward_slope(source, target, slope, rows, bias_base=None):
        for r in range(0, rows, 16):
            value, grad = gelu_both(biased(source, r, bias_base))
            target[r : r + 16, :] = value.astype(B16)
            slope[r : r + 16, :] = grad

    def policy(hidden, noise):
        out = dot_nn(wht_a[...].astype(B16), hidden) + lanes_of(hb[0:48, :])
        eps = jnp.concatenate([noise, jnp.zeros((24 - ACT, rt), F32)], axis=0)
        tl = jnp.tanh(out[24:48])
        ls = tl - 1.0
        spread = jnp.exp(ls) * eps
        u = out[0:24] + spread
        act = jnp.tanh(u)
        soft = jnp.maximum(-2.0 * u, 0.0) + jnp.log(1.0 + jnp.exp(-jnp.abs(2.0 * u)))
        terms = -0.5 * eps * eps - ls - HALF_LOG_TAU - 2.0 * (LOG_TWO - u - soft)
        keep = lax.broadcasted_iota(jnp.int32, (24, rt), 0) < ACT
        logp = jnp.sum(jnp.where(keep, terms, 0.0), axis=0, keepdims=True)
        return act, logp, tl, spread

    def head(net, hidden):
        rows = slice(net * 8, net * 8 + 8)
        return dot_nn(wht_c[rows, :].astype(B16), hidden) + lanes_of(hb[48 + net * 8 : 56 + net * 8, :])

    def back_second(source, slope, target, first, last):
        for r in range(first, last, 16):
            d_pre = source[r : r + 16, :] * slope[r : r + 16, :]
            target[r : r + 16, :] = d_pre.astype(B16)
            acc_b[r : r + 16, :] += lane_sum(d_pre)

    def back_first(source, slope, target, first, last):
        for r in range(first, last, 16):
            target[r : r + 16, :] = (source[r : r + 16, :] * slope[r : r + 16, :]).astype(B16)

    def stages(sub):
        cols = slice(sub * rt, sub * rt + rt)
        xn, xd, xq = xn_all.at[sub], xd_all.at[sub], xq_all.at[sub]
        z1, z1q, z2, z2q, zn, zt = (r.at[sub] for r in (z1_all, z1q_all, z2_all, z2q_all, zn_all, zt_all))
        h1n, h2n, h1, h2 = (r.at[sub] for r in (h1n_all, h2n_all, h1_all, h2_all))
        h1q, h2q, h1t, h2t = (r.at[sub] for r in (h1q_all, h2q_all, h1t_all, h2t_all))
        g1, g1q, g2 = (r.at[sub] for r in (g1_all, g1q_all, g2_all))
        dz1, dz2, dzq1, dzq2 = (r.at[sub] for r in (dz1_all, dz2_all, dzq1_all, dzq2_all))

        xn[0:OBS, :] = next_ref[:, cols]
        xd[0:OBS, :] = obs_ref[:, cols]
        xq[0:OBS, :] = obs_ref[:, cols]
        xd[OBS : OBS + ACT, :] = action_ref[:, cols]
        zn[...] = dot_nn(w1t[0:H, :], xn[...])
        z1[...] = dot_nn(w1t[0 : 3 * H, :], xd[...])
        yield
        forward(zn, h1n, H)
        forward_slope(z1, h1, g1, 3 * H)
        yield
        zn[...] = dot_nn(w2t[0:H, :], h1n[...])
        for net in range(3):
            rows = slice(net * H, net * H + H)
            z2[rows, :] = dot_nn(w2t[rows, :], h1[rows, :])
        forward(zn, h2n, H, 0)
        forward_slope(z2, h2, g2, 3 * H, 0)
        yield
        index = t_index * (n_steps * subs * rt) + (step * subs + sub) * rt
        index = index + lax.broadcasted_iota(jnp.int32, (1, rt), 1)
        valid = (index < count_ref[0]).astype(F32)
        alpha = jnp.exp(jnp.full((1, rt), state_ref[0], F32))
        omega = state_ref[3] * state_ref[3]
        act_next, logp_next, _, _ = policy(h2n[...], next_noise_ref[:, cols])
        act_new, logp_new, tl_new, spread_new = policy(h2[0:H, :], noise_ref[:, cols])
        xn[OBS : OBS + ACT, :] = act_next[0:ACT].astype(B16)
        xq[OBS : OBS + ACT, :] = act_new[0:ACT].astype(B16)
        zt[...] = dot_nn(w1t[3 * H : 5 * H, :], xn[...])
        z1q[...] = dot_nn(w1t[H : 3 * H, :], xq[...])
        yield
        forward(zt, h1t, 2 * H)
        forward_slope(z1q, h1q, g1q, 2 * H)
        yield
        for net in range(2):
            rows = slice(net * H, net * H + H)
            zt[rows, :] = dot_nn(w2t[(3 + net) * H : (4 + net) * H, :], h1t[rows, :])
            z2q[rows, :] = dot_nn(w2t[(1 + net) * H : (2 + net) * H, :], h1q[rows, :])
        forward(zt, h2t, 2 * H, 3 * H)
        for r in range(0, 2 * H, 16):
            value, grad = gelu_both(biased(z2q, r, H))
            h2q[r : r + 16, :] = value.astype(B16)
            dzq2[r : r + 16, :] = (lanes_of(wqb[r : r + 16, :]) * grad).astype(B16)
        yield
        out_t = [head(2 + net, h2t[net * H : net * H + H, :])[0:1] for net in range(2)]
        out_d = [head(net, h2[(1 + net) * H : (2 + net) * H, :]) for net in range(2)]
        out_q = [head(net, h2q[net * H : net * H + H, :])[0:1] for net in range(2)]
        for net in range(2):
            rows = slice(net * H, net * H + H)
            z1q[rows, :] = dot_nn(w2[(1 + net) * H : (2 + net) * H, :], dzq2[rows, :])
        alive = 1.0 - terminal_ref[:, cols].astype(F32)
        target = reward_ref[:, cols] + GAMMA * alive * (jnp.minimum(out_t[0], out_t[1]) - alpha * logp_next)
        loss_row = valid * (alpha * logp_new - 0.5 * (out_q[0] + out_q[1]))
        sigma_row = jnp.zeros((1, rt), F32)
        next_row = valid * (logp_next - ACT)
        d_heads = []
        for net in range(2):
            log_sigma = jnp.tanh(out_d[net][1:2])
            sigma = jnp.exp(log_sigma)
            error = target - out_d[net][0:1]
            inverse = 1.0 / (sigma * sigma)
            scaled = error * inverse
            square = error * scaled
            loss_row = loss_row + valid * (omega * (0.5 * square + log_sigma))
            sigma_row = sigma_row + valid * sigma
            d_q = -(omega * valid) * scaled
            d_s = (omega * valid) * (1.0 - square) * (1.0 - log_sigma * log_sigma)
            d_heads.append(jnp.concatenate([d_q, d_s, jnp.zeros((6, rt), F32)], axis=0).astype(B16))
        acc_s[64:65, :] += lane_sum(loss_row)
        acc_s[72:73, :] += lane_sum(sigma_row)
        acc_s[80:81, :] += lane_sum(next_row)
        yield
        for net in range(2):
            rows = slice((1 + net) * H, (2 + net) * H)
            acc_s[48 + net * 8 : 56 + net * 8, :] += lane_sum(d_heads[net].astype(F32))
            acc_hc[net * 8 : net * 8 + 8, :] += dot_nt(d_heads[net], h2[rows, :])
            z2[rows, :] = dot_nn(wh_c[:, net * 8 : net * 8 + 8], d_heads[net])
        back_first(z1q, g1q, dzq1, 0, 2 * H)
        d_act = dot_nn(w1a[0:32, :], dzq1[0:H, :]) + dot_nn(w1a[32:64, :], dzq1[H : 2 * H, :])
        back_second(z2, g2, dz2, H, 3 * H)
        yield
        d_act = d_act[0:24] * (-0.5 * valid)
        d_logp = alpha * valid
        d_u = d_act * (1.0 - act_new * act_new) + (2.0 * d_logp) * act_new
        d_ls = (d_u * spread_new - d_logp) * (1.0 - tl_new * tl_new)
        d_out = jnp.concatenate([d_u, d_ls], axis=0).astype(B16)
        acc_s[0:48, :] += lane_sum(d_out.astype(F32))
        acc_ha[...] += dot_nt(d_out, h2[0:H, :])
        z2[0:H, :] = dot_nn(wh_a[...], d_out)
        for net in range(1, 3):
            rows = slice(net * H, net * H + H)
            z1[rows, :] = dot_nn(w2[rows, :], dz2[rows, :])
        back_second(z2, g2, dz2, 0, H)
        z1[0:H, :] = dot_nn(w2[0:H, :], dz2[0:H, :])
        back_first(z1, g1, dz1, H, 3 * H)
        yield
        back_first(z1, g1, dz1, 0, H)
        for net in (1, 2, 0):
            rows = slice(net * H, net * H + H)
            acc2[rows, :] += dot_nt(h1[rows, :], dz2[rows, :])
        acc1[...] += dot_nt(xd[0:K_USE, :], dz1[...])

    running = [stages(sub) for sub in range(subs)]
    alive_count = subs
    turn = 0
    done = [False] * subs
    while alive_count:
        for sub in range(subs):
            if not done[sub] and turn >= sub * offset:
                if next(running[sub], "end") == "end":
                    done[sub] = True
                    alive_count -= 1
        turn += 1

    @pl.when(step == n_steps - 1)
    def _():
        mine, others = own_chunk(orders), own_chunk(orders[::-1])
        flat[:, FLAT_SMALL:FLAT_ROWS, :] = jnp.zeros((2, FLAT_ROWS - FLAT_SMALL, 128), F32)
        flat[:, FLAT_AW1 - 8 : FLAT_AW1, :] = jnp.zeros((2, 8, 128), F32)
        flat[:, FLAT_AW2 - 8 : FLAT_AW2, :] = jnp.zeros((2, 8, 128), F32)
        sums = jnp.sum(jnp.transpose(acc_s[...]), axis=0, keepdims=True)
        lane = lax.broadcasted_iota(jnp.int32, (1, 128), 1)
        keep = (lane < ACT) | ((lane >= 24) & (lane < 24 + ACT)) | ((lane >= 48) & (lane < 50))
        keep = keep | ((lane >= 56) & (lane < 58)) | (lane == LANE_LOSS) | (lane == LANE_SIGMA) | (lane == LANE_NEXT)
        sums = jnp.where(keep, sums, 0.0)
        sums = jnp.where(lane == LANE_COUNT, 0.5 * count_ref[0].astype(F32), sums)
        for side in range(2):
            lanes = slice(side * HALF, side * HALF + HALF)
            for net in range(2):
                columns = slice((1 + net) * H + side * HALF, (1 + net) * H + side * HALF + HALF)
                flat[side, pl.ds(FLAT_CW1 + net, C_IN, stride=2), :] = acc1[0:C_IN, columns]
            flat[side, FLAT_AW1 : FLAT_AW1 + OBS, :] = acc1[0:OBS, lanes]
            flat[side, FLAT_AW1 + OBS : FLAT_AW1 + A_IN, :] = acc1[BIAS_ROW : BIAS_ROW + 1, lanes]
            for net in range(3):
                rows = slice(net * H + side * HALF, net * H + side * HALF + HALF)
                for part in range(2):
                    base = FLAT_AW2 + (net * 2 + part) * HALF
                    flat[side, base : base + HALF, :] = acc2[rows, part * 128 : part * 128 + 128]
            for part in range(2):
                cols = slice(part * 128, part * 128 + 128)
                base = FLAT_AHEAD + part * 40
                flat[side, base : base + ACT, :] = acc_ha[0:ACT, cols]
                flat[side, base + ACT : base + 2 * ACT, :] = acc_ha[24 : 24 + ACT, cols]
                for net in range(2):
                    base = FLAT_CHEAD + part * 4 + net * 2
                    flat[side, base : base + 2, :] = acc_hc[net * 8 : net * 8 + 2, cols]
            for net in range(3):
                for part in range(2):
                    rows = slice(net * H + part * 128, net * H + part * 128 + 128)
                    row = FLAT_B2 + part * 4 + net
                    flat[side, row : row + 1, :] = jnp.sum(jnp.transpose(acc_b[rows, :]), axis=0, keepdims=True)
            flat[side, FLAT_SUMS : FLAT_SUMS + 1, :] = sums
        size = FLAT_ROWS // len(order)
        per = len(order) // n_own
        for place, rel in enumerate(order):
            start = pl.multiple_of(jnp.bitwise_xor(mine, rel) * size, size)
            own_outs[place // per][(place % per) * size : (place % per) * size + size, :] = flat[0, pl.ds(start, size), :]
            start = pl.multiple_of(jnp.bitwise_xor(others, rel) * size, size)
            par_out[place * size : place * size + size, :] = flat[1, pl.ds(start, size), :]


SUB_ROWS = 256
SUBS = 2
SUB_OFFSET = 2


def run_step(groups, arrays, pack_own, pack_par, small, count, state, when):
    obs, next_obs, action, noise, next_noise, reward, terminal = arrays
    rows = obs.shape[1] // groups["tensor"]
    rt = min(SUB_ROWS, rows)
    subs = min(SUBS, rows // rt)
    steps = rows // (rt * subs)
    order, n_own = groups["order"], groups["first"]

    def tile(height):
        return pl.BlockSpec((height, rt * subs), lambda i: (0, lax.axis_index("tensor") * steps + i))

    def each(height, dtype):
        return VMEM((subs, height, rt), dtype)

    whole = pl.BlockSpec(memory_space=VMEM)
    smem = pl.BlockSpec(memory_space=pltpu.SMEM)
    scratch = [
        VMEM((5 * H, K_PAD), B16), VMEM((5 * H, H), B16), VMEM((5 * H, H), B16), VMEM((64, H), B16),
        VMEM((48, H), F32), VMEM((H, 48), B16), VMEM((32, H), F32), VMEM((H, 32), B16),
        VMEM((80, 128), F32), VMEM((5 * H, 128), F32), VMEM((2 * H, 128), F32),
        each(K_PAD, B16), each(K_PAD, B16), each(K_PAD, B16),
        each(3 * H, F32), each(2 * H, F32), each(3 * H, F32), each(2 * H, F32), each(H, F32), each(2 * H, F32),
        each(H, B16), each(H, B16), each(3 * H, B16), each(3 * H, B16),
        each(2 * H, B16), each(2 * H, B16), each(2 * H, B16), each(2 * H, B16),
        each(3 * H, F32), each(2 * H, F32), each(3 * H, F32),
        each(3 * H, B16), each(3 * H, B16), each(2 * H, B16), each(2 * H, B16),
        VMEM((K_USE, 3 * H), F32), VMEM((3 * H, H), F32), VMEM((48, H), F32), VMEM((16, H), F32),
        VMEM((3 * H, 128), F32), VMEM((128, 128), F32), VMEM((2, FLAT_ROWS, 128), F32),
    ]
    outs = [jax.ShapeDtypeStruct((FLAT_ROWS // n_own, 128), F32)] * n_own + [jax.ShapeDtypeStruct((FLAT_ROWS, 128), F32)]
    outs = outs + [jax.ShapeDtypeStruct((8, 128), F32)]
    return pl.pallas_call(
        functools.partial(step_kernel, rt, subs, SUB_OFFSET, order, groups["orders"], n_own),
        grid=(steps,),
        in_specs=[smem, smem, smem, tile(OBS), tile(OBS), tile(ACT), tile(ACT), tile(ACT), tile(1), tile(1)] + [whole] * 7,
        out_specs=[whole] * (n_own + 2),
        out_shape=outs,
        scratch_shapes=scratch,
        compiler_params=pltpu.CompilerParams(vmem_limit_bytes=STEP_VMEM),
        name="step",
    )(
        count, *in_hbm(state), when, *in_hbm(obs, next_obs, action, noise, next_noise, reward, terminal),
        pack_own, pack_par, *in_hbm(*small),
    )


def last_sum_kernel(size, n_in, orders, *refs):
    out = refs[n_in]
    first = own_chunk(orders) * size
    part = jnp.zeros((8, 128), F32)
    lane = lax.broadcasted_iota(jnp.int32, (8, 128), 1)
    for r in range(0, size, 8):
        total = refs[0][r : r + 8, :]
        for ref in refs[1:n_in]:
            total = total + ref[r : r + 8, :]
        out[r : r + 8, :] = total
        row = first + r + lax.broadcasted_iota(jnp.int32, (8, 128), 0)
        weight = jnp.where(row < FLAT_SMALL, 1.0, 0.5)
        weight = jnp.where((row >= FLAT_SUMS) & (lane >= LANE_LOSS), 0.0, weight)
        part = part + total * total * weight
    out[size : size + 8, :] = part


def last_sum(values, orders):
    size = values[0].shape[0]
    return pl.pallas_call(
        functools.partial(last_sum_kernel, size, len(values), orders),
        out_shape=jax.ShapeDtypeStruct((size + 8, 128), F32),
        compiler_params=pltpu.CompilerParams(vmem_limit_bytes=SMALL_VMEM),
        name="lastsum",
    )(*values)


AT_ONCE = 64


def update_kernel(order, orders, n_parts, sizes, *refs):
    parts = refs[:n_parts]
    (
        square_own, square_other, fix_ref, state_ref,
        a_w1, a_w1_m, a_w2, a_w2_m, a_head, a_head_m,
        c_w1, c_w1_m, c_w2, c_w2_m, c_head, c_head_m, bias2, bias2_m,
        t_w1, t_w2, t_head, t_bias2,
        o_a_w1, o_a_w1_f, o_a_w1_s, o_a_w2, o_a_w2_f, o_a_w2_s, o_a_head, o_a_head_f, o_a_head_s,
        o_c_w1, o_c_w1_f, o_c_w1_s, o_c_w2, o_c_w2_f, o_c_w2_s, o_c_head, o_c_head_f, o_c_head_s,
        o_bias2, o_bias2_f, o_bias2_s, o_scalars, o_norm,
        flat, rows_new, rows_target,
    ) = refs[n_parts:]
    size, stride = sizes
    mine = own_chunk(orders)
    per = len(order) // n_parts
    square = square_own[...] + square_other[...]
    for place, rel in enumerate(order):
        start = pl.multiple_of(jnp.bitwise_xor(mine, rel) * size, size)
        base = (place % per) * stride
        flat[pl.ds(start, size), :] = parts[place // per][base : base + size, :]
    sums = flat[FLAT_SUMS : FLAT_SUMS + 1, :]
    lane = lax.broadcasted_iota(jnp.int32, (1, 128), 1)

    def pick(index):
        return jnp.sum(jnp.where(lane == index, sums, 0.0), axis=1, keepdims=True)

    loss_sum, sigma_sum, next_sum, count = (pick(i) for i in (LANE_LOSS, LANE_SIGMA, LANE_NEXT, LANE_COUNT))
    inverse = 1.0 / count
    total = jnp.sum(jnp.sum(square, axis=0, keepdims=True), axis=1, keepdims=True)
    norm = jnp.sqrt(total) * inverse
    clip = jnp.minimum(1.0, CLIP / (norm + 1e-06))
    scale = clip * inverse
    unfix_one, unfix_two = fix_ref[0:1, 0:1], fix_ref[1:2, 0:1]

    def adam(weight, first, second, grad, decay=DECAY):
        first = BETA_ONE * first + (1.0 - BETA_ONE) * grad
        second = BETA_TWO * second + (1.0 - BETA_TWO) * (grad * grad)
        step = first * unfix_one / (jnp.sqrt(second * unfix_two) + ADAM_EPS)
        if decay:
            step = step + decay * weight
        return weight - RATE * step, first, second

    def polyak(target, new):
        return (1.0 - RHO) * target + RHO * new

    moments = a_w1_m.reshape(2 * A_IN, 128)
    for r in range(0, A_IN, AT_ONCE):
        n = min(AT_ONCE, A_IN - r)
        rows = slice(r, r + n)
        new, first, second = adam(
            a_w1[rows, :], moments[pl.ds(2 * r, n, stride=2), :], moments[pl.ds(2 * r + 1, n, stride=2), :],
            flat[FLAT_AW1 + r : FLAT_AW1 + r + n, :] * scale,
        )
        o_a_w1[rows, :] = new
        o_a_w1_f[rows, :] = first
        o_a_w1_s[rows, :] = second
    for net in range(3):
        for part in range(2):
            lanes = slice(part * 128, part * 128 + 128)
            base = FLAT_AW2 + (net * 2 + part) * HALF
            grad = flat[base : base + HALF, :] * scale
            if net == 0:
                new, first, second = adam(a_w2[:, lanes], a_w2_m[0, :, lanes], a_w2_m[1, :, lanes], grad)
                o_a_w2[:, lanes] = new
                o_a_w2_f[:, lanes] = first
                o_a_w2_s[:, lanes] = second
            else:
                c = net - 1
                new, first, second = adam(c_w2[c, :, lanes], c_w2_m[0, c, :, lanes], c_w2_m[1, c, :, lanes], grad)
                o_c_w2[c, :, lanes] = new
                o_c_w2[2 + c, :, lanes] = polyak(t_w2[c, :, lanes], new)
                o_c_w2_f[c, :, lanes] = first
                o_c_w2_s[c, :, lanes] = second
    both = 2 * C_IN
    for r in range(0, both, AT_ONCE):
        rows = slice(r, min(r + AT_ONCE, both))
        new, first, second = adam(
            c_w1.reshape(both, 128)[rows, :], c_w1_m.at[0].reshape(both, 128)[rows, :],
            c_w1_m.at[1].reshape(both, 128)[rows, :], flat[rows, :] * scale,
        )
        o_c_w1_f.reshape(both, 128)[rows, :] = first
        o_c_w1_s.reshape(both, 128)[rows, :] = second
        rows_new[rows, :] = new
        rows_target[rows, :] = polyak(t_w1.reshape(both, 128)[rows, :], new)
    four = o_c_w1.reshape(2 * both, 128)
    for c in range(2):
        four[pl.ds(c, C_IN, stride=4), :] = rows_new[pl.ds(c, C_IN, stride=2), :]
        four[pl.ds(2 + c, C_IN, stride=4), :] = rows_target[pl.ds(c, C_IN, stride=2), :]
    columns = jnp.transpose(jnp.broadcast_to(sums, (128, 128)))
    bias_a = jnp.concatenate([columns[0:ACT, 0:1], columns[24 : 24 + ACT, 0:1]], axis=0)
    grad = jnp.concatenate(
        [flat[FLAT_AHEAD : FLAT_AHEAD + 2 * ACT, :], flat[FLAT_AHEAD + 40 : FLAT_AHEAD + 40 + 2 * ACT, :], bias_a], axis=1
    )
    new, first, second = adam(a_head[...], a_head_m[:, 0, :], a_head_m[:, 1, :], grad * scale)
    o_a_head[...] = new
    o_a_head_f[...] = first
    o_a_head_s[...] = second
    for c in range(2):
        rows = slice(FLAT_CHEAD + c * 2, FLAT_CHEAD + c * 2 + 2)
        rows_b = slice(FLAT_CHEAD + 4 + c * 2, FLAT_CHEAD + 6 + c * 2)
        bias_c = columns[LANE_C + 8 * c : LANE_C + 8 * c + 2, 0:1]
        grad = jnp.concatenate([flat[rows, :], flat[rows_b, :], bias_c], axis=1) * scale
        new, first, second = adam(c_head[c], c_head_m[0, c], c_head_m[1, c], grad)
        o_c_head[c] = new
        o_c_head[2 + c] = polyak(t_head[c], new)
        o_c_head_f[c] = first
        o_c_head_s[c] = second
    grad = jnp.concatenate([flat[FLAT_B2 : FLAT_B2 + 3, :], flat[FLAT_B2 + 4 : FLAT_B2 + 7, :]], axis=1) * scale
    new, first, second = adam(bias2[...], bias2_m[:, 0, :], bias2_m[:, 1, :], grad)
    o_bias2[0:3, :] = new
    o_bias2[3:5, :] = polyak(t_bias2[...], new[1:3])
    o_bias2_f[...] = first
    o_bias2_s[...] = second
    log_alpha = jnp.full((1, 1), state_ref[0], F32)
    g_alpha = -next_sum
    new, first, second = adam(
        log_alpha, jnp.full((1, 1), state_ref[1], F32), jnp.full((1, 1), state_ref[2], F32), g_alpha * inverse, 0.0
    )
    stat = (1.0 - TAU_STAT) * state_ref[3] + TAU_STAT * sigma_sum / (2.0 * count)
    loss = (loss_sum + log_alpha * g_alpha) * inverse
    for place, value in enumerate((new, first, second, stat, loss)):
        o_scalars[place] = value[0, 0]
    o_norm[0] = norm[0, 0]


def shards(
    groups, obs, action, next_obs, reward, terminal, noise, next_noise, counts, step_count,
    a_w1, a_w2, a_head, c_w1, c_w2, c_head, bias2, tc_w1, tc_w2, tc_head, tc_bias2,
    a_w1_mom, a_w2_mom, a_head_mom, c_w1_mom, c_w2_mom, c_head_mom, bias2_mom, state,
):
    n_dp = groups["dp"]
    swap = [(0, 1), (1, 0)]

    def partner(value):
        return lax.ppermute(value, "tensor", swap)

    def across(value, phase, k):
        masks = [sum(((k >> place) & 1) << bit for place, bit in enumerate(bits)) for bits in phase]
        pairs = [(2 * d + t, 2 * (d ^ masks[t]) + t) for d in range(n_dp) for t in range(2)]
        return lax.ppermute(value, ("dp", "tensor"), pairs)

    tr = jnp.transpose
    c_w1v, tc_w1v = tr(c_w1, (1, 0, 2)), tr(tc_w1, (1, 0, 2))
    a_headv, c_headv, tc_headv = tr(a_head), tr(c_head, (0, 2, 1)), tr(tc_head, (0, 2, 1))
    pack = pack_weights(a_w1, c_w1v, tc_w1v, a_w2, c_w2, tc_w2)
    pack_par = partner(pack)
    arrays = (
        tr(obs), tr(next_obs), tr(action), tr(noise), tr(next_noise), reward.reshape(1, -1), terminal.reshape(1, -1),
    )
    small = (a_headv, c_headv, tc_headv, bias2, tc_bias2)
    outs = run_step(groups, arrays, pack, pack_par, small, counts, state, step_count)
    own, par, fixes = outs[:-2], outs[-2], outs[-1]
    received = partner(par)
    size = FLAT_ROWS // len(own)
    values = [item + received[i * size : i * size + size] for i, item in enumerate(own)]

    *scatters, last = groups["phases"]
    following = [1 << len(phase[0]) for phase in scatters[1:]] + [1]
    for phase, ways_next in zip(scatters, following):
        got = [values[0]] + [across(values[k], phase, k) for k in range(1, 1 << len(phase[0]))]
        size = got[0].shape[0] // ways_next
        values = [sum(item[j * size : j * size + size] for item in got) for j in range(ways_next)]
    got = [values[0]] + [across(values[0], last, k) for k in range(1, 1 << len(last[0]))]
    block = last_sum(got, groups["orders"])
    for number, phase in reversed(list(enumerate(scatters))):
        got = [block] + [across(block, phase, k) for k in range(1, 1 << len(phase[0]))]
        if number:
            block = jnp.concatenate(got)
    parts = got
    own_square = sum(
        part[r + size : r + size + 8] for part in parts for r in range(0, part.shape[0], size + 8)
    )
    other_square = partner(own_square)

    sds = jax.ShapeDtypeStruct
    shapes = [
        (A_IN, HALF)] * 3 + [(HALF, H)] * 3 + [(2 * ACT, H + 1)] * 3 + [
        (C_IN, 4, HALF), (C_IN, 2, HALF), (C_IN, 2, HALF),
        (4, HALF, H), (2, HALF, H), (2, HALF, H),
        (4, 2, H + 1), (2, 2, H + 1), (2, 2, H + 1),
        (5, H), (3, H), (3, H), (5,), (1,),
    ]
    whole = pl.BlockSpec(memory_space=VMEM)
    smem = pl.BlockSpec(memory_space=pltpu.SMEM)
    res = pl.pallas_call(
        functools.partial(update_kernel, groups["order"], groups["orders"], len(parts), (size, size + 8)),
        in_specs=[whole] * (len(parts) + 3) + [smem] + [whole] * 18,
        out_specs=[whole] * 21 + [smem, smem],
        out_shape=[sds(s, F32) for s in shapes],
        scratch_shapes=[VMEM((FLAT_ROWS, 128), F32), VMEM((2 * C_IN, 128), F32), VMEM((2 * C_IN, 128), F32)],
        compiler_params=pltpu.CompilerParams(vmem_limit_bytes=UPDATE_VMEM),
        name="update",
    )(
        *parts, own_square, other_square, fixes, state,
        a_w1, tr(a_w1_mom, (1, 0, 2)), a_w2, a_w2_mom, a_headv, tr(a_head_mom, (2, 0, 1)),
        c_w1v, tr(c_w1_mom, (0, 2, 1, 3)), c_w2, c_w2_mom, c_headv, tr(c_head_mom, (0, 1, 3, 2)),
        bias2, tr(bias2_mom, (1, 0, 2)), tc_w1v, tc_w2, tc_headv, tc_bias2,
    )
    res = list(res)
    for place in (6, 7, 8):
        res[place] = tr(res[place])
    for place in (9, 10, 11):
        res[place] = tr(res[place], (1, 0, 2))
    for place in (15, 16, 17):
        res[place] = tr(res[place], (0, 2, 1))
    return tuple(res)


def plan(mesh):
    n_dp = mesh.shape["dp"]
    bits = n_dp.bit_length() - 1
    assert n_dp == 1 << bits and mesh.shape["tensor"] == 2
    groups = [tuple(range(low, min(low + 2, bits))) for low in range(0, bits, 2)]
    assert len(groups) > 1
    pairs = [group for group in groups if len(group) == 2]
    turned = pairs[1:] + pairs[:1] + groups[len(pairs) :]
    phases = list(zip(groups, turned))
    order = [0]
    low = 0
    for group in groups[:-1]:
        order = [rel | (k << low) for rel in order for k in range(1 << len(group))]
        low += len(group)
    return {
        "dp": n_dp,
        "tensor": mesh.shape["tensor"],
        "phases": phases,
        "order": tuple(order),
        "orders": tuple(tuple(bit for group in core[:-1] for bit in group) for core in (groups, turned)),
        "first": 1 << len(groups[0]),
    }


def solution(mesh):
    in_specs = (
        P("dp", None), P("dp", None), P("dp", None), P("dp"), P("dp"), P("dp", None), P("dp", None), P("dp"), P(),
        P(None, "tensor"), P("tensor", None), P(), P(None, None, "tensor"), P(None, "tensor", None), P(), P(),
        P(None, None, "tensor"), P(None, "tensor", None), P(), P(),
        P(None, None, "tensor"), P(None, "tensor", None), P(), P(None, None, None, "tensor"),
        P(None, None, "tensor", None), P(), P(), P(),
    )
    out_specs = (
        P(None, "tensor"), P(None, "tensor"), P(None, "tensor"),
        P("tensor", None), P("tensor", None), P("tensor", None),
        P(), P(), P(),
        P(None, None, "tensor"), P(None, None, "tensor"), P(None, None, "tensor"),
        P(None, "tensor", None), P(None, "tensor", None), P(None, "tensor", None),
        P(), P(), P(), P(), P(), P(), P(), P(),
    )
    return jax.shard_map(
        functools.partial(shards, plan(mesh)), mesh=mesh, in_specs=in_specs, out_specs=out_specs, check_vma=False
    )
```
